128 devices in a mesh: req: 4 (over y), tp: 32 (over x, z, core).
Axes of the slice: x: 4, y: 4, z: 4, core: 2. Of those that a mesh axis runs over, the one named last changes fastest.
Arguments:
- hidden_states: bfloat16 [16, 4, 1024], P('req'), may hold values from -48 to 48
- lengths: int32 [16], P('req'), may hold values from 16 to 4096, as said below
- qkv_weight: bfloat16 [2048, 1024], P('tp'), may hold values from -1 to 1
- rotated_key_cache: bfloat16 [16, 4096, 512], P('req', 'tp'), may hold values from -1000 to 1000
- earlier_value_cache: bfloat16 [16, 4096, 512], P('req', 'tp'), may hold values from -16 to 16
- out_weight: bfloat16 [1024, 1024], P('tp'), may hold values from -0.1875 to 0.1875
- expert_ids: int32 [16, 4, 8], P('req'), may hold values from 0 to 31, all different within a row
- combine_weights: int32 [16, 4, 8], P('req'), may hold values from 4096 to 65535
- gate_up_weight: bfloat16 [32, 1024, 1024], P('tp'), may hold values from -0.1875 to 0.1875
- down_weight: bfloat16 [32, 512, 1024], P('tp'), may hold values from -0.25 to 0.25
Outputs:
- layer_output: bfloat16 [16, 4, 1024], P('req')
The draws below stay inside these ranges and needn't reach their ends.
Inputs may be any that keep to these rules, and one draw needn't show every extreme that they name: `lengths`: cache length of each request; some request has exactly 4096. `expert_ids`: each token's 8 experts are distinct.
All inputs are finite; a program needn't handle non-finite values.
Results may differ from the reference program's by a relative error of at most 0.008.
Values may be sent and summed in bfloat16 or wider, within the bound.
A program may use at most 64 MiB of HBM per device.

```python
from functools import partial
import jax
import jax.numpy as jnp
from jax import lax

D = 1024
QUERY_HEADS = 16
KEY_VALUE_HEADS = 8
HEAD_DIMENSION = 64
FF = 512
EXPERTS = 32
TOPK = 8
DECODE_STEPS = 4
CACHE_POSITIONS = 4096
REQUEST_TOTAL = 16
QKV = 2048
N_TP = 32


def length_table(key):
    base_key = jax.random.fold_in(key, 11)
    first_key, second_key, third_key = jax.random.split(base_key, 3)
    spread = jax.random.randint(first_key, (REQUEST_TOTAL,), 0, CACHE_POSITIONS - 15, dtype=jnp.int32)
    shifts = jax.random.randint(second_key, (REQUEST_TOTAL,), 0, 8, dtype=jnp.int32)
    value_rows = 16 + jnp.right_shift(spread, shifts)
    longest = jax.random.randint(third_key, (), 0, REQUEST_TOTAL, dtype=jnp.int32)
    return jnp.where(jnp.arange(REQUEST_TOTAL, dtype=jnp.int32) == longest, CACHE_POSITIONS, value_rows).astype(jnp.int32)


def hidden_table(key):
    base_key = jax.random.fold_in(key, 12)
    first_key, second_key = jax.random.split(base_key, 2)
    columns = jnp.exp(jax.random.uniform(second_key, (D,), jnp.float32, jnp.log(0.33), jnp.log(3.0)))
    random_jitter = jax.random.truncated_normal(first_key, -4.0, 4.0, (REQUEST_TOTAL, DECODE_STEPS, D), jnp.float32)
    return jnp.clip(random_jitter * columns, -48.0, 48.0)


def projection_table(key):
    base_key = jax.random.fold_in(key, 13)
    value_rows = jax.random.truncated_normal(base_key, -4.0, 4.0, (QKV, D), jnp.float32) * D ** (-0.5)
    return jnp.clip(value_rows, -1.0, 1.0)


def draw_hidden_states(key, part):
    return hidden_table(key).astype(jnp.bfloat16)


def draw_lengths(key, part):
    return length_table(key)


def draw_qkv_weight(key, part):
    return projection_table(key).astype(jnp.bfloat16)


def draw_rotated_key_cache(key, part):
    base_key = jax.random.fold_in(key, 14)
    first_key, second_key = jax.random.split(base_key, 2)
    random_jitter = jax.random.truncated_normal(first_key, -4.0, 4.0, (REQUEST_TOTAL, CACHE_POSITIONS, KEY_VALUE_HEADS * HEAD_DIMENSION), jnp.float32)
    scales = jnp.exp(jax.random.uniform(second_key, (REQUEST_TOTAL, CACHE_POSITIONS, 1), jnp.float32, jnp.log(0.3), jnp.log(3.0)))
    key_rows = random_jitter * scales
    return jnp.clip(key_rows, -1000.0, 1000.0).astype(jnp.bfloat16)


def draw_earlier_value_cache(key, part):
    base_key = jax.random.fold_in(key, 15)
    first_key, second_key = jax.random.split(base_key, 2)
    band_length = max(1, CACHE_POSITIONS // 32)
    rough_scores = jax.random.truncated_normal(second_key, -4.0, 4.0, (REQUEST_TOTAL, CACHE_POSITIONS // band_length, 1, KEY_VALUE_HEADS * HEAD_DIMENSION), jnp.float32)
    random_jitter = jax.random.truncated_normal(first_key, -4.0, 4.0, (REQUEST_TOTAL, CACHE_POSITIONS // band_length, band_length, KEY_VALUE_HEADS * HEAD_DIMENSION), jnp.float32)
    value_rows = random_jitter + 2.0 * rough_scores
    return jnp.clip(value_rows.reshape(REQUEST_TOTAL, CACHE_POSITIONS, KEY_VALUE_HEADS * HEAD_DIMENSION), -16.0, 16.0).astype(jnp.bfloat16)


def place_ends(drawn, own_key, least, high):
    place = [jax.random.randint(jax.random.fold_in(own_key, axis), (), 0, length) for axis, length in enumerate(drawn.shape)]
    widest = drawn.shape.index(max(drawn.shape))
    neighbour = place[:widest] + [(place[widest] + 1) % drawn.shape[widest]] + place[widest + 1:]
    return drawn.at[tuple(place)].set(least).at[tuple(neighbour)].set(high)


def block_levels(own_key, extent, pieces, low, largest):
    level, own = 1.0, jax.random.fold_in(own_key, 6)
    for dim, parts in pieces:
        heights = jnp.exp(jax.random.uniform(jax.random.fold_in(own, dim), (parts,), jnp.float32, low / len(pieces), largest / len(pieces)))
        level = level * jnp.repeat(heights, extent[dim] // parts).reshape([-1 if axis == dim else 1 for axis in range(len(extent))])
    return level


def choose_distinct(stream_key, rows, count, top, lift):
    sequence = jax.random.permutation(jax.random.fold_in(stream_key, 1), count)
    pull = sequence
    for power in range(3):
        pull = pull * pull // count
    pull = pull * lift // count
    chance = jax.random.randint(jax.random.fold_in(stream_key, 2), (rows, count), 0, 4096) + pull
    fixed_rows = jax.random.permutation(jax.random.fold_in(stream_key, 3), rows)[jnp.arange(count) % rows]
    chance = jnp.where(jnp.arange(rows)[:, None] == fixed_rows[None, :], 1 << 14, chance)
    priority = chance * count + jnp.arange(count)
    return lax.top_k(priority.astype(jnp.int32), top)[1].astype(jnp.int32)


def noise(key, extent, deviation, limit, shards=(), kind=jnp.bfloat16):
    values = jax.random.normal(key, extent, jnp.float32) * deviation
    if len(shards) > 0:
        values = block_levels(key, extent, shards, -0.22, 0.18) * values
    return jnp.clip(values, min=-limit, max=limit).astype(kind)


def setup_inputs(seed: int = 0) -> dict:
    key_of = jax.random.split(jax.random.key(seed), 11)
    return {
        "hidden_states": draw_hidden_states(jax.random.fold_in(key_of[10], 71), 0),
        "lengths": draw_lengths(jax.random.fold_in(key_of[10], 71), 0),
        "qkv_weight": draw_qkv_weight(jax.random.fold_in(key_of[10], 71), 0),
        "rotated_key_cache": draw_rotated_key_cache(jax.random.fold_in(key_of[10], 71), 0),
        "earlier_value_cache": draw_earlier_value_cache(jax.random.fold_in(key_of[10], 71), 0),
        "out_weight": noise(key_of[5], (QUERY_HEADS * HEAD_DIMENSION, D), (QUERY_HEADS * HEAD_DIMENSION) ** -0.5, 0.1875, ((0, 32),)),
        "expert_ids": choose_distinct(key_of[6], REQUEST_TOTAL * DECODE_STEPS, EXPERTS, TOPK, 2048).reshape((REQUEST_TOTAL, DECODE_STEPS, TOPK)),
        "combine_weights": place_ends(jax.random.randint(key_of[7], (REQUEST_TOTAL, DECODE_STEPS, TOPK), 4096, 65536), jax.random.fold_in(key_of[7], 1), 4096, 65535).astype(jnp.int32),
        "gate_up_weight": noise(key_of[8], (EXPERTS, D, 2 * FF), D ** -0.5, 0.1875, ((0, 32),)),
        "down_weight": noise(key_of[9], (EXPERTS, FF, D), FF ** -0.5, 0.25, ((0, 32),)),
    }


EPSILON = 1e-05
ROPE_BASE = 10000.0
NEGATIVE = -1e+30

def rms_rows(value_rows):
    return value_rows * lax.rsqrt(lax.optimization_barrier(jnp.mean(value_rows * value_rows, axis=-1, keepdims=True)) + EPSILON)

def apply_rotation(value_rows, position_index):
    half_width = value_rows.shape[-1] // 2
    rates = ROPE_BASE ** (-2.0 * jnp.arange(half_width, dtype=jnp.float32) / value_rows.shape[-1])
    angles = position_index[:, None, None] * rates
    cosine = jnp.cos(angles)
    sines = jnp.sin(angles)
    front_half = value_rows[..., :half_width]
    back_half = value_rows[..., half_width:]
    return jnp.concatenate([front_half * cosine - back_half * sines, back_half * cosine + front_half * sines], axis=-1)

def attend_one(item, qkv_weight):
    tokens, length, key_rows, value_rows = item
    query_total_width = QUERY_HEADS * HEAD_DIMENSION
    key_value_width = KEY_VALUE_HEADS * HEAD_DIMENSION
    group_count = QUERY_HEADS // KEY_VALUE_HEADS
    normed = rms_rows(tokens.astype(jnp.float32)).astype(jnp.bfloat16)
    projected_rows = jnp.dot(normed, qkv_weight.T, preferred_element_type=jnp.float32).astype(jnp.bfloat16)
    position_index = (length + jnp.arange(DECODE_STEPS, dtype=jnp.int32)).astype(jnp.float32)
    query_rows = apply_rotation(projected_rows[:, :query_total_width].reshape(DECODE_STEPS, QUERY_HEADS, HEAD_DIMENSION).astype(jnp.float32), position_index).astype(jnp.bfloat16)
    fresh_keys = apply_rotation(projected_rows[:, query_total_width:query_total_width + key_value_width].reshape(DECODE_STEPS, KEY_VALUE_HEADS, HEAD_DIMENSION).astype(jnp.float32), position_index).astype(jnp.bfloat16)
    fresh_values = projected_rows[:, query_total_width + key_value_width:].reshape(DECODE_STEPS, KEY_VALUE_HEADS, HEAD_DIMENSION).astype(jnp.float32)
    grouped_rows = query_rows.reshape(DECODE_STEPS, KEY_VALUE_HEADS, group_count, HEAD_DIMENSION).transpose(1, 0, 2, 3).reshape(KEY_VALUE_HEADS, DECODE_STEPS * group_count, HEAD_DIMENSION).astype(jnp.float32)
    block_extent = CACHE_POSITIONS // N_TP
    stored_keys = key_rows.reshape(N_TP, block_extent, KEY_VALUE_HEADS, HEAD_DIMENSION).astype(jnp.float32)
    stored_values = value_rows.reshape(N_TP, block_extent, KEY_VALUE_HEADS, HEAD_DIMENSION).astype(jnp.float32)
    score_scale = HEAD_DIMENSION ** (-0.5)
    scores = jnp.einsum('gqd,ncgd->ngqc', grouped_rows, stored_keys) * score_scale
    live_mask = (jnp.arange(CACHE_POSITIONS, dtype=jnp.int32) < length).reshape(N_TP, 1, 1, block_extent)
    masked = jnp.where(live_mask, scores, NEGATIVE)
    highest = lax.optimization_barrier(jnp.max(masked, axis=-1))
    weights = jnp.where(live_mask, jnp.exp(masked - highest[..., None]), 0.0)
    weight_sum = lax.optimization_barrier(jnp.sum(weights, axis=-1))
    rounded = lax.optimization_barrier(weights.astype(jnp.bfloat16)).astype(jnp.float32)
    value_sum = jnp.einsum('ngqc,ncgd->ngqd', rounded, stored_values)
    top_score = lax.optimization_barrier(jnp.max(highest, axis=0))
    rescale = jnp.exp(highest - top_score)
    total_all = lax.optimization_barrier(jnp.sum(weight_sum * rescale, axis=0))
    sum_all = lax.optimization_barrier(jnp.sum(value_sum * rescale[..., None], axis=0))
    new_scores = jnp.einsum('gqd,sgd->gqs', grouped_rows, fresh_keys.astype(jnp.float32)) * score_scale
    query_step = jnp.arange(DECODE_STEPS * group_count, dtype=jnp.int32) // group_count
    causal = jnp.arange(DECODE_STEPS, dtype=jnp.int32)[None, :] <= query_step[:, None]
    new_masked = jnp.where(causal, new_scores, NEGATIVE)
    final_peak = jnp.maximum(top_score, lax.optimization_barrier(jnp.max(new_masked, axis=-1)))
    new_weights = jnp.where(causal, jnp.exp(new_masked - final_peak[..., None]), 0.0)
    carried = jnp.exp(top_score - final_peak)
    denominator = total_all * carried + lax.optimization_barrier(jnp.sum(new_weights, axis=-1))
    new_rounded = lax.optimization_barrier(new_weights.astype(jnp.bfloat16)).astype(jnp.float32)
    numerator = sum_all * carried[..., None] + jnp.einsum('gqs,sgd->gqd', new_rounded, fresh_values)
    final_result = numerator / denominator[..., None]
    return final_result.reshape(KEY_VALUE_HEADS, DECODE_STEPS, group_count, HEAD_DIMENSION).transpose(1, 0, 2, 3).reshape(DECODE_STEPS, query_total_width).astype(jnp.bfloat16)

def reference(hidden_states, lengths, qkv_weight, rotated_key_cache, earlier_value_cache, out_weight, expert_ids, combine_weights, gate_up_weight, down_weight):
    attended = lax.map(partial(attend_one, qkv_weight=qkv_weight), (hidden_states, lengths, rotated_key_cache, earlier_value_cache))
    token_count = REQUEST_TOTAL * DECODE_STEPS
    projected_rows = jnp.dot(attended.reshape(token_count, QUERY_HEADS * HEAD_DIMENSION), out_weight, preferred_element_type=jnp.float32)
    residual = hidden_states.reshape(token_count, D).astype(jnp.float32) + projected_rows
    normed_second = rms_rows(residual).astype(jnp.bfloat16)
    shares = combine_weights.reshape(token_count, TOPK).astype(jnp.float32) / 65536.0
    chosen = expert_ids.reshape(token_count, TOPK)

    def add_expert(running, item):
        expert_index, gate_up, down_part = item
        united_out = jnp.dot(normed_second, gate_up, preferred_element_type=jnp.float32)
        activation = (jax.nn.silu(united_out[:, :FF]) * united_out[:, FF:]).astype(jnp.bfloat16)
        outcome = jnp.dot(activation, down_part, preferred_element_type=jnp.float32)
        factors = lax.optimization_barrier(jnp.sum(jnp.where(chosen == expert_index, shares, 0.0), axis=-1))
        return (running + factors[:, None] * outcome, None)
    mixture, _ = lax.scan(add_expert, jnp.zeros((token_count, D), jnp.float32), (jnp.arange(EXPERTS, dtype=jnp.int32), gate_up_weight, down_weight))
    return (residual + mixture).astype(jnp.bfloat16).reshape(REQUEST_TOTAL, DECODE_STEPS, D)
```

```python
import functools

import jax
import jax.numpy as jnp
import numpy as np
from jax import lax
from jax.experimental import pallas as pl
from jax.experimental.pallas import tpu as pltpu
from jax.sharding import PartitionSpec as P

EPSILON = 1e-05
ROPE_BASE = 10000.0
NEGATIVE = -1e30
MESH = pl.DeviceIdType.MESH
F32 = jnp.float32
BF16 = jnp.bfloat16


def hops(offset):
    return min(offset, 4 - offset)


PEERS = sorted(
    [(dx, dz, dc) for dx in range(4) for dz in range(4) for dc in range(2) if dx or dz or dc],
    key=lambda o: -(hops(o[0]) + hops(o[1]) + 0.5 * o[2]),
)


def stack_rows(pieces):
    return jnp.concatenate(pieces, axis=0)


def kernel(
    hidden_h, lengths_h, qkv_h, keys_h, values_h, outw_h, ids_h, comb_h, gate_h, down_h, rates_h,
    out_h,
    hidden_v, lengths_s, qkv_v, keys_v, values_v, ids_v, comb_v, gate_v, down_v, rates_v,
    qsend, qbuf, wbuf, asend, abuf, psend, pbuf, rsend, rbuf, msend, mbuf, osend,
    lsem, ssem, rsem,
):
    me = lax.axis_index("tp")
    x = lax.div(me, 8)
    z = lax.rem(lax.div(me, 2), 4)
    c = lax.rem(me, 2)
    g_me = 2 * x + c

    def device(offset):
        dx, dz, dc = offset
        px = lax.rem(x + dx, 4) if dx else x
        pz = lax.rem(z + dz, 4) if dz else z
        pc = lax.rem(c + dc, 2) if dc else c
        return px, pz, pc

    def index(offset):
        px, pz, pc = device(offset)
        return px * 8 + pz * 2 + pc

    peers = [index(o) for o in PEERS]

    barrier = pltpu.get_barrier_semaphore()
    for p in peers:
        pl.semaphore_signal(barrier, inc=1, device_id={"tp": p}, device_id_type=MESH)

    def load(src, dst, i):
        copy = pltpu.make_async_copy(src, dst, lsem.at[i])
        copy.start()
        return copy

    c_hidden = load(hidden_h, hidden_v, 0)
    c_len = load(lengths_h, lengths_s, 1)
    c_qkv0 = load(qkv_h, qkv_v.at[pl.ds(0, 64)], 2)
    c_qkv1 = load(qkv_h, qkv_v.at[pl.ds(64, 64)], 3)
    c_rates = load(rates_h, rates_v, 4)
    c_keys = load(keys_h, keys_v, 5)
    c_values = load(values_h, values_v, 6)
    c_ids = load(ids_h, ids_v, 7)
    c_comb = load(comb_h, comb_v, 8)
    c_gate = load(gate_h.at[0], gate_v, 9)
    c_down = load(down_h.at[0], down_v, 10)

    def send(src, dst, phase, p):
        pltpu.make_async_remote_copy(
            src_ref=src, dst_ref=dst, send_sem=ssem.at[phase], recv_sem=rsem.at[phase],
            device_id={"tp": p}, device_id_type=MESH,
        ).start()

    def wait_bytes(ref, sem):
        pltpu.make_async_copy(ref, ref, sem).wait()

    sub = lax.broadcasted_iota(jnp.int32, (8, 128), 0)
    lane = lax.broadcasted_iota(jnp.int32, (8, 128), 1)
    low_half = lane < 64
    top_rows = sub < 4

    c_hidden.wait()
    rows = stack_rows([hidden_v[r].astype(F32) for r in range(4)])
    normed = (
        rows * lax.rsqrt(jnp.mean(rows * rows, axis=-1, keepdims=True) + EPSILON)
    ).astype(BF16)
    c_len.wait()
    lens = [lengths_s[r] for r in range(4)]
    c_rates.wait()
    front = jnp.where(top_rows, lens[0], lens[1])
    rear = jnp.where(top_rows, lens[2], lens[3])
    position = (jnp.where(low_half, front, rear) + jnp.bitwise_and(sub, 3)).astype(F32)
    angles = position * rates_v[...]
    cosine = jnp.cos(angles)
    sine = jnp.sin(angles)
    c_qkv0.wait()
    c_qkv1.wait()
    head = lax.dot_general(
        normed, qkv_v[...], (((1,), (1,)), ((), ())), preferred_element_type=F32
    )
    head = head.astype(BF16).astype(F32)
    packed = jnp.where(low_half, head[0:8], head[8:16])
    ahead = pltpu.roll(packed, 96, 1)
    behind = pltpu.roll(packed, 32, 1)
    first = jnp.bitwise_and(lane, 63) < 32
    turned = packed * cosine + jnp.where(first, -ahead, behind) * sine
    scale = jnp.where(me < 16, 0.125, 1.0).astype(F32)
    rotated = jnp.broadcast_to(me, (8, 128)) < 24
    qsend[...] = jnp.where(rotated, turned.astype(BF16).astype(F32) * scale, packed).astype(BF16)

    pl.semaphore_wait(barrier, 31)
    for p in peers:
        send(qsend, qbuf.at[me], 0, p)
    pltpu.make_async_copy(qsend, qbuf.at[me], rsem.at[0]).start()

    slot = 2 * lax.rem(z, 2) + c
    owner_core = lax.div(z, 2)
    for dz in (2, 1, 3):
        send(outw_h, wbuf.at[slot], 1, x * 8 + lax.rem(z + dz, 4) * 2 + owner_core)

    @pl.when(owner_core == c)
    def _():
        pltpu.make_async_copy(outw_h, wbuf.at[slot], rsem.at[1]).start()

    @pl.when(owner_core != c)
    def _():
        send(outw_h, wbuf.at[slot], 1, x * 8 + z * 2 + owner_core)

    wait_bytes(qbuf, rsem.at[0])
    heads = [qbuf[h].astype(F32) for h in range(16)]
    mixed = []
    for g in range(8):
        e, f = heads[2 * g], heads[2 * g + 1]
        mixed.append(
            (
                jnp.where(top_rows, e, pltpu.roll(f, 4, 0)),
                jnp.where(top_rows, pltpu.roll(e, 4, 0), f),
            )
        )
    c_keys.wait()
    c_values.wait()
    zero = jnp.zeros((8, 128), F32)
    cell = lax.broadcasted_iota(jnp.int32, (64, 128), 1) + me * 128
    for r in range(4):
        blocks = []
        for g in range(8):
            u = mixed[g][r % 2]
            if r // 2 != g % 2:
                u = pltpu.roll(u, 64, 1)
            blocks.append(jnp.where(low_half if g % 2 == 0 else ~low_half, u, 0.0))
        columns = [
            jnp.concatenate([blocks[g] if g // 2 == k else zero for g in range(8)], axis=0)
            for k in range(4)
        ]
        queries = jnp.concatenate(columns, axis=1).astype(BF16)
        scores = lax.dot_general(
            queries, keys_v[r], (((1,), (1,)), ((), ())), preferred_element_type=F32
        )
        live = cell < lens[r]
        masked = jnp.where(live, scores, NEGATIVE)
        peak = jnp.max(masked, axis=-1, keepdims=True)
        weights = jnp.where(live, jnp.exp(masked - peak), 0.0)
        total = jnp.sum(weights, axis=-1, keepdims=True)
        sums = jnp.dot(weights.astype(BF16), values_v[r], preferred_element_type=F32)
        for g in range(8):
            o = sums[8 * g : 8 * g + 8, (g // 2) * 128 : (g // 2) * 128 + 128]
            if g % 2:
                o = pltpu.roll(o, 64, 1)
            stats = jnp.where(
                lane < 96,
                jnp.broadcast_to(peak[8 * g : 8 * g + 8], (8, 128)),
                jnp.broadcast_to(total[8 * g : 8 * g + 8], (8, 128)),
            )
            asend[(g // 2) * 8 + r * 2 + g % 2] = jnp.where(low_half, o, stats)

    for p in peers:
        send(asend.at[p], abuf.at[me], 2, p)
    pltpu.make_async_copy(asend.at[me], abuf.at[me], rsem.at[2]).start()

    late = jnp.broadcast_to(lax.rem(z, 2), (8, 128)) == 1
    rear_half = jnp.broadcast_to(lax.div(z, 2), (8, 128)) == 1
    e = qbuf[2 * g_me].astype(F32)
    f = qbuf[2 * g_me + 1].astype(F32)
    u = jnp.where(
        late,
        jnp.where(top_rows, pltpu.roll(e, 4, 0), f),
        jnp.where(top_rows, e, pltpu.roll(f, 4, 0)),
    )
    own_queries = jnp.where(low_half, jnp.where(rear_half, pltpu.roll(u, 64, 1), u), 0.0)

    def own_rows(i):
        v = qbuf[i].astype(F32)
        v = jnp.where(rear_half, pltpu.roll(v, 64, 1), v)
        return jnp.where(late, pltpu.roll(v, 4, 0), v)

    new_keys = own_rows(16 + g_me)
    new_values = own_rows(24 + g_me)
    step = jnp.bitwise_and(sub, 3)
    new_scores = []
    for s in range(4):
        score = jnp.sum(
            own_queries * jnp.broadcast_to(new_keys[s : s + 1], (8, 128)), axis=-1, keepdims=True
        )
        new_scores.append(
            jnp.where(step >= s, jnp.broadcast_to(score, (8, 128)), NEGATIVE)
        )
    new_peak = functools.reduce(jnp.maximum, new_scores)
    new_weights = [jnp.exp(v - new_peak) for v in new_scores]
    new_total = functools.reduce(jnp.add, new_weights)
    new_sum = functools.reduce(
        jnp.add,
        [
            new_weights[s].astype(BF16).astype(F32)
            * jnp.broadcast_to(new_values[s : s + 1], (8, 128))
            for s in range(4)
        ],
    )
    c_ids.wait()
    c_comb.wait()
    factors = [
        jnp.sum(
            jnp.where(ids_v[r] == me, comb_v[r], 0).astype(F32), axis=-1, keepdims=True
        )
        * (1.0 / 65536.0)
        for r in range(4)
    ]
    wait_bytes(wbuf, rsem.at[1])

    wait_bytes(abuf, rsem.at[2])
    peaks = [jnp.broadcast_to(abuf[b][:, 64:65], (8, 128)) for b in range(32)]
    top = functools.reduce(jnp.maximum, peaks + [new_peak])
    total_all = jnp.zeros((8, 128), F32)
    for b in range(32):
        total_all = total_all + jnp.exp(peaks[b] - top) * abuf[b]
    carried = jnp.exp(new_peak - top)
    denominator = jnp.broadcast_to(total_all[:, 96:97], (8, 128)) + carried * new_total
    attended = jnp.where(low_half, (total_all + carried * new_sum) / denominator, 0.0)
    attended = jnp.where(top_rows, attended, pltpu.roll(attended, 64, 1)).astype(BF16)
    product = jnp.dot(
        attended, wbuf[...].reshape(128, 1024), preferred_element_type=F32
    )
    product = product[0:4] + product[4:8]
    for k in range(8):
        psend[k] = product[:, k * 128 : k * 128 + 128]
    row_peers = [o for o in PEERS if o[1] == 0]
    for o in row_peers:
        px, _, pc = device(o)
        send(psend.at[2 * px + pc], pbuf.at[g_me], 3, index(o))
    pltpu.make_async_copy(psend.at[g_me], pbuf.at[g_me], rsem.at[3]).start()

    own_column = pl.multiple_of(g_me * 128, 128)
    own_hidden = hidden_v[z, :, pl.ds(own_column, 128)].astype(F32)
    wait_bytes(pbuf, rsem.at[3])
    residual = own_hidden + jnp.sum(pbuf[...], axis=0)
    rsend[...] = residual
    for p in peers:
        send(rsend, rbuf.at[g_me, z], 4, p)
    pltpu.make_async_copy(rsend, rbuf.at[g_me, z], rsem.at[4]).start()
    c_gate.wait()
    c_down.wait()
    wait_bytes(rbuf, rsem.at[4])
    rows = jnp.concatenate(
        [stack_rows([rbuf[k, r] for r in range(4)]) for k in range(8)], axis=1
    )
    normed = (
        rows * lax.rsqrt(jnp.mean(rows * rows, axis=-1, keepdims=True) + EPSILON)
    ).astype(BF16)
    united = jnp.dot(normed, gate_v[...], preferred_element_type=F32)
    gate = united[:, :512]
    activation = (gate / (1.0 + jnp.exp(-gate)) * united[:, 512:]).astype(BF16)
    outcome = jnp.dot(activation, down_v[...], preferred_element_type=F32)
    for r in range(4):
        share = outcome[4 * r : 4 * r + 4] * factors[r]
        for g in range(8):
            msend[(g // 2) * 8 + r * 2 + g % 2] = share[:, g * 128 : g * 128 + 128].astype(BF16)
    for p in peers:
        send(msend.at[p], mbuf.at[me], 5, p)
    pltpu.make_async_copy(msend.at[me], mbuf.at[me], rsem.at[5]).start()
    wait_bytes(mbuf, rsem.at[5])
    osend[...] = (residual + jnp.sum(mbuf[...].astype(F32), axis=0)).astype(BF16)
    target = out_h.at[z, :, pl.ds(own_column, 128)]
    for p in peers:
        send(osend, target, 6, p)
    pltpu.make_async_copy(osend, target, rsem.at[6]).start()
    wait_bytes(out_h, rsem.at[6])

    wait_bytes(qbuf.at[pl.ds(0, 31)], ssem.at[0])
    wait_bytes(wbuf.at[pl.ds(0, 3)], ssem.at[1])

    @pl.when(owner_core != c)
    def _():
        wait_bytes(wbuf.at[0], ssem.at[1])

    wait_bytes(abuf.at[pl.ds(0, 31)], ssem.at[2])
    wait_bytes(pbuf.at[pl.ds(0, 7)], ssem.at[3])
    wait_bytes(qbuf.at[pl.ds(0, 31)], ssem.at[4])
    wait_bytes(mbuf.at[pl.ds(0, 31)], ssem.at[5])
    wait_bytes(mbuf.at[pl.ds(0, 31)], ssem.at[6])


def per_device(*args):
    half = np.arange(128) % 32
    rates = np.broadcast_to(
        (ROPE_BASE ** (-2.0 * half / 64.0)).astype(np.float32)[None, :], (8, 128)
    )
    anywhere = pl.BlockSpec(memory_space=pl.ANY)
    return pl.pallas_call(
        kernel,
        out_shape=jax.ShapeDtypeStruct((4, 4, 1024), BF16),
        in_specs=[anywhere] * 11,
        out_specs=anywhere,
        scratch_shapes=[
            pltpu.VMEM((4, 4, 1024), BF16),
            pltpu.SMEM((4,), jnp.int32),
            pltpu.VMEM((128, 1024), BF16),
            pltpu.VMEM((4, 128, 512), BF16),
            pltpu.VMEM((4, 128, 512), BF16),
            pltpu.VMEM((4, 4, 8), jnp.int32),
            pltpu.VMEM((4, 4, 8), jnp.int32),
            pltpu.VMEM((1024, 1024), BF16),
            pltpu.VMEM((512, 1024), BF16),
            pltpu.VMEM((8, 128), F32),
            pltpu.VMEM((8, 128), BF16),
            pltpu.VMEM((32, 8, 128), BF16),
            pltpu.VMEM((4, 32, 1024), BF16),
            pltpu.VMEM((32, 8, 128), F32),
            pltpu.VMEM((32, 8, 128), F32),
            pltpu.VMEM((8, 4, 128), F32),
            pltpu.VMEM((8, 4, 128), F32),
            pltpu.VMEM((4, 128), F32),
            pltpu.VMEM((8, 4, 4, 128), F32),
            pltpu.VMEM((32, 4, 128), BF16),
            pltpu.VMEM((32, 4, 128), BF16),
            pltpu.VMEM((4, 128), BF16),
            pltpu.SemaphoreType.DMA((11,)),
            pltpu.SemaphoreType.DMA((7,)),
            pltpu.SemaphoreType.DMA((7,)),
        ],
        compiler_params=pltpu.CompilerParams(collective_id=0, has_side_effects=True),
        name="decoder_layer",
    )(*args, jnp.asarray(rates))


def solution(mesh):
    in_specs = (
        P("req", None, None),
        P("req"),
        P("tp", None),
        P("req", "tp", None),
        P("req", "tp", None),
        P("tp", None),
        P("req", None, None),
        P("req", None, None),
        P("tp", None, None),
        P("tp", None, None),
    )
    out_specs = P("req", None, None)
    return jax.shard_map(
        per_device, mesh=mesh, in_specs=in_specs, out_specs=out_specs, check_vma=False
    )
```

```python
import functools

import jax
import jax.numpy as jnp
import numpy as np
from jax import lax
from jax.experimental import pallas as pl
from jax.experimental.pallas import tpu as pltpu
from jax.sharding import PartitionSpec as P

EPSILON = 1e-05
ROPE_BASE = 10000.0
NEGATIVE = -1e30
MESH = pl.DeviceIdType.MESH
F32 = jnp.float32
BF16 = jnp.bfloat16


def hops(offset):
    return min(offset, 4 - offset)


PEERS = sorted(
    [(dx, dz, dc) for dx in range(4) for dz in range(4) for dc in range(2) if dx or dz or dc],
    key=lambda o: -(hops(o[0]) + hops(o[1]) + 0.5 * o[2]),
)


def stack_rows(pieces):
    return jnp.concatenate(pieces, axis=0)


def kernel(
    hidden_h, lengths_h, qkv_h, keys_h, values_h, outw_h, ids_h, comb_h, gate_h, down_h, rates_h,
    out_h,
    hidden_v, lengths_s, qkv_v, keys_v, values_v, ids_v, comb_v, gate_v, down_v, rates_v,
    qsend, qbuf, wbuf, asend, abuf, psend, pbuf, rsend, rbuf, msend, mbuf, osend,
    lsem, ssem, rsem,
):
    me = lax.axis_index("tp")
    x = lax.div(me, 8)
    z = lax.rem(lax.div(me, 2), 4)
    c = lax.rem(me, 2)
    g_me = 2 * x + c

    def device(offset):
        dx, dz, dc = offset
        px = lax.rem(x + dx, 4) if dx else x
        pz = lax.rem(z + dz, 4) if dz else z
        pc = lax.rem(c + dc, 2) if dc else c
        return px, pz, pc

    def index(offset):
        px, pz, pc = device(offset)
        return px * 8 + pz * 2 + pc

    peers = [index(o) for o in PEERS]

    barrier = pltpu.get_barrier_semaphore()
    for p in peers:
        pl.semaphore_signal(barrier, inc=1, device_id={"tp": p}, device_id_type=MESH)

    def load(src, dst, i):
        copy = pltpu.make_async_copy(src, dst, lsem.at[i])
        copy.start()
        return copy

    c_hidden = load(hidden_h, hidden_v, 0)
    c_len = load(lengths_h, lengths_s, 1)
    c_qkv0 = load(qkv_h, qkv_v.at[pl.ds(0, 64)], 2)
    c_qkv1 = load(qkv_h, qkv_v.at[pl.ds(64, 64)], 3)
    c_rates = load(rates_h, rates_v, 4)
    c_keys = load(keys_h, keys_v, 5)
    c_values = load(values_h, values_v, 6)
    c_ids = load(ids_h, ids_v, 7)
    c_comb = load(comb_h, comb_v, 8)
    c_gate = load(gate_h.at[0], gate_v, 9)
    c_down = load(down_h.at[0], down_v, 10)

    def send(src, dst, phase, p):
        pltpu.make_async_remote_copy(
            src_ref=src, dst_ref=dst, send_sem=ssem.at[phase], recv_sem=rsem.at[phase],
            device_id={"tp": p}, device_id_type=MESH,
        ).start()

    def wait_bytes(ref, sem):
        pltpu.make_async_copy(ref, ref, sem).wait()

    sub = lax.broadcasted_iota(jnp.int32, (8, 128), 0)
    lane = lax.broadcasted_iota(jnp.int32, (8, 128), 1)
    low_half = lane < 64
    top_rows = sub < 4

    c_hidden.wait()
    rows = stack_rows([hidden_v[r].astype(F32) for r in range(4)])
    normed = (
        rows * lax.rsqrt(jnp.mean(rows * rows, axis=-1, keepdims=True) + EPSILON)
    ).astype(BF16)
    c_len.wait()
    lens = [lengths_s[r] for r in range(4)]
    c_rates.wait()
    front = jnp.where(top_rows, lens[0], lens[1])
    rear = jnp.where(top_rows, lens[2], lens[3])
    position = (jnp.where(low_half, front, rear) + jnp.bitwise_and(sub, 3)).astype(F32)
    angles = position * jnp.broadcast_to(rates_v[...], (8, 128))
    cosine = jnp.cos(angles)
    sine = jnp.sin(angles)
    c_qkv0.wait()
    c_qkv1.wait()
    head = lax.dot_general(
        normed, qkv_v[...], (((1,), (1,)), ((), ())), preferred_element_type=F32
    )
    head = head.astype(BF16).astype(F32)
    packed = jnp.where(low_half, head[0:8], head[8:16])
    ahead = pltpu.roll(packed, 96, 1)
    behind = pltpu.roll(packed, 32, 1)
    first = jnp.bitwise_and(lane, 63) < 32
    turned = packed * cosine + jnp.where(first, -ahead, behind) * sine
    scale = jnp.where(me < 16, 0.125, 1.0).astype(F32)
    rotated = jnp.broadcast_to(me, (8, 128)) < 24
    qsend[...] = jnp.where(rotated, turned.astype(BF16).astype(F32) * scale, packed).astype(BF16)

    pl.semaphore_wait(barrier, 31)
    for p in peers:
        send(qsend, qbuf.at[me], 0, p)
    pltpu.make_async_copy(qsend, qbuf.at[me], rsem.at[0]).start()

    slot = 2 * lax.rem(z, 2) + c
    owner_core = lax.div(z, 2)
    for dz in (2, 1, 3):
        send(outw_h, wbuf.at[slot], 1, x * 8 + lax.rem(z + dz, 4) * 2 + owner_core)

    @pl.when(owner_core == c)
    def _():
        pltpu.make_async_copy(outw_h, wbuf.at[slot], rsem.at[1]).start()

    @pl.when(owner_core != c)
    def _():
        send(outw_h, wbuf.at[slot], 1, x * 8 + z * 2 + owner_core)

    wait_bytes(qbuf, rsem.at[0])
    heads = [qbuf[h].astype(F32) for h in range(16)]
    mixed = []
    for g in range(8):
        e, f = heads[2 * g], heads[2 * g + 1]
        mixed.append(
            (
                jnp.where(top_rows, e, pltpu.roll(f, 4, 0)),
                jnp.where(top_rows, pltpu.roll(e, 4, 0), f),
            )
        )
    c_keys.wait()
    c_values.wait()
    zero = jnp.zeros((8, 128), F32)
    cell = lax.broadcasted_iota(jnp.int32, (64, 128), 1) + me * 128
    for r in range(4):
        blocks = []
        for g in range(8):
            u = mixed[g][r % 2]
            if r // 2 != g % 2:
                u = pltpu.roll(u, 64, 1)
            blocks.append(jnp.where(low_half if g % 2 == 0 else ~low_half, u, 0.0))
        columns = [
            jnp.concatenate([blocks[g] if g // 2 == k else zero for g in range(8)], axis=0)
            for k in range(4)
        ]
        queries = jnp.concatenate(columns, axis=1).astype(BF16)
        scores = lax.dot_general(
            queries, keys_v[r], (((1,), (1,)), ((), ())), preferred_element_type=F32
        )
        live = cell < lens[r]
        masked = jnp.where(live, scores, NEGATIVE)
        peak = jnp.max(masked, axis=-1, keepdims=True)
        weights = jnp.where(live, jnp.exp(masked - peak), 0.0)
        total = jnp.sum(weights, axis=-1, keepdims=True)
        sums = jnp.dot(weights.astype(BF16), values_v[r], preferred_element_type=F32)
        for g in range(8):
            o = sums[8 * g : 8 * g + 8, (g // 2) * 128 : (g // 2) * 128 + 128]
            if g % 2:
                o = pltpu.roll(o, 64, 1)
            stats = jnp.where(
                lane < 96,
                jnp.broadcast_to(peak[8 * g : 8 * g + 8], (8, 128)),
                jnp.broadcast_to(total[8 * g : 8 * g + 8], (8, 128)),
            )
            asend[(g // 2) * 8 + r * 2 + g % 2] = jnp.where(low_half, o, stats)

    for p in peers:
        send(asend.at[p], abuf.at[me], 2, p)
    pltpu.make_async_copy(asend.at[me], abuf.at[me], rsem.at[2]).start()

    late = jnp.broadcast_to(lax.rem(z, 2), (8, 128)) == 1
    rear_half = jnp.broadcast_to(lax.div(z, 2), (8, 128)) == 1
    e = qbuf[2 * g_me].astype(F32)
    f = qbuf[2 * g_me + 1].astype(F32)
    u = jnp.where(
        late,
        jnp.where(top_rows, pltpu.roll(e, 4, 0), f),
        jnp.where(top_rows, e, pltpu.roll(f, 4, 0)),
    )
    own_queries = jnp.where(low_half, jnp.where(rear_half, pltpu.roll(u, 64, 1), u), 0.0)

    def own_rows(i):
        v = qbuf[i].astype(F32)
        v = jnp.where(rear_half, pltpu.roll(v, 64, 1), v)
        return jnp.where(late, pltpu.roll(v, 4, 0), v)

    new_keys = own_rows(16 + g_me)
    new_values = own_rows(24 + g_me)
    step = jnp.bitwise_and(sub, 3)
    new_scores = []
    for s in range(4):
        score = jnp.sum(
            own_queries * jnp.broadcast_to(new_keys[s : s + 1], (8, 128)), axis=-1, keepdims=True
        )
        new_scores.append(
            jnp.where(step >= s, jnp.broadcast_to(score, (8, 128)), NEGATIVE)
        )
    new_peak = functools.reduce(jnp.maximum, new_scores)
    new_weights = [jnp.exp(v - new_peak) for v in new_scores]
    new_total = functools.reduce(jnp.add, new_weights)
    new_sum = functools.reduce(
        jnp.add,
        [
            new_weights[s].astype(BF16).astype(F32)
            * jnp.broadcast_to(new_values[s : s + 1], (8, 128))
            for s in range(4)
        ],
    )
    c_ids.wait()
    c_comb.wait()
    factors = [
        jnp.sum(
            jnp.where(ids_v[r] == me, comb_v[r], 0).astype(F32), axis=-1, keepdims=True
        )
        * (1.0 / 65536.0)
        for r in range(4)
    ]
    wait_bytes(wbuf, rsem.at[1])

    wait_bytes(abuf, rsem.at[2])
    peaks = [jnp.broadcast_to(abuf[b][:, 64:65], (8, 128)) for b in range(32)]
    top = functools.reduce(jnp.maximum, peaks + [new_peak])
    total_all = jnp.zeros((8, 128), F32)
    for b in range(32):
        total_all = total_all + jnp.exp(peaks[b] - top) * abuf[b]
    carried = jnp.exp(new_peak - top)
    denominator = jnp.broadcast_to(total_all[:, 96:97], (8, 128)) + carried * new_total
    attended = jnp.where(low_half, (total_all + carried * new_sum) / denominator, 0.0)
    attended = jnp.where(top_rows, attended, pltpu.roll(attended, 64, 1)).astype(BF16)
    product = jnp.dot(
        attended, wbuf[...].reshape(128, 1024), preferred_element_type=F32
    )
    product = product[0:4] + product[4:8]
    for k in range(8):
        psend[k] = product[:, k * 128 : k * 128 + 128]
    row_peers = [o for o in PEERS if o[1] == 0]
    for o in row_peers:
        px, _, pc = device(o)
        send(psend.at[2 * px + pc], pbuf.at[g_me], 3, index(o))
    pltpu.make_async_copy(psend.at[g_me], pbuf.at[g_me], rsem.at[3]).start()

    own_column = pl.multiple_of(g_me * 128, 128)
    own_hidden = hidden_v[z, :, pl.ds(own_column, 128)].astype(F32)
    wait_bytes(pbuf, rsem.at[3])
    residual = own_hidden + jnp.sum(pbuf[...], axis=0)
    rsend[...] = residual
    for p in peers:
        send(rsend, rbuf.at[g_me, z], 4, p)
    pltpu.make_async_copy(rsend, rbuf.at[g_me, z], rsem.at[4]).start()
    c_gate.wait()
    c_down.wait()
    wait_bytes(rbuf, rsem.at[4])
    rows = jnp.concatenate(
        [stack_rows([rbuf[k, r] for r in range(4)]) for k in range(8)], axis=1
    )
    normed = (
        rows * lax.rsqrt(jnp.mean(rows * rows, axis=-1, keepdims=True) + EPSILON)
    ).astype(BF16)
    united = jnp.dot(normed, gate_v[...], preferred_element_type=F32)
    gate = united[:, :512]
    activation = (gate / (1.0 + jnp.exp(-gate)) * united[:, 512:]).astype(BF16)
    outcome = jnp.dot(activation, down_v[...], preferred_element_type=F32)
    for r in range(4):
        share = outcome[4 * r : 4 * r + 4] * factors[r]
        for g in range(8):
            msend[(g // 2) * 8 + r * 2 + g % 2] = share[:, g * 128 : g * 128 + 128].astype(BF16)
    for p in peers:
        send(msend.at[p], mbuf.at[me], 5, p)
    pltpu.make_async_copy(msend.at[me], mbuf.at[me], rsem.at[5]).start()
    wait_bytes(mbuf, rsem.at[5])
    osend[...] = (residual + jnp.sum(mbuf[...].astype(F32), axis=0)).astype(BF16)
    target = out_h.at[z, :, pl.ds(own_column, 128)]
    for p in peers:
        send(osend, target, 6, p)
    pltpu.make_async_copy(osend, target, rsem.at[6]).start()
    wait_bytes(out_h, rsem.at[6])

    wait_bytes(qbuf.at[pl.ds(0, 31)], ssem.at[0])
    wait_bytes(wbuf.at[pl.ds(0, 3)], ssem.at[1])

    @pl.when(owner_core != c)
    def _():
        wait_bytes(wbuf.at[0], ssem.at[1])

    wait_bytes(abuf.at[pl.ds(0, 31)], ssem.at[2])
    wait_bytes(pbuf.at[pl.ds(0, 7)], ssem.at[3])
    wait_bytes(qbuf.at[pl.ds(0, 31)], ssem.at[4])
    wait_bytes(mbuf.at[pl.ds(0, 31)], ssem.at[5])
    wait_bytes(mbuf.at[pl.ds(0, 31)], ssem.at[6])


def per_device(*args):
    half = np.arange(128) % 32
    rates = (ROPE_BASE ** (-2.0 * half / 64.0)).astype(np.float32)
    anywhere = pl.BlockSpec(memory_space=pl.ANY)
    return pl.pallas_call(
        kernel,
        out_shape=pltpu.VMEM((4, 4, 1024), BF16),
        in_specs=[anywhere] * 11,
        out_specs=pl.BlockSpec(memory_space=pltpu.VMEM),
        scratch_shapes=[
            pltpu.VMEM((4, 4, 1024), BF16),
            pltpu.SMEM((4,), jnp.int32),
            pltpu.VMEM((128, 1024), BF16),
            pltpu.VMEM((4, 128, 512), BF16),
            pltpu.VMEM((4, 128, 512), BF16),
            pltpu.VMEM((4, 4, 8), jnp.int32),
            pltpu.VMEM((4, 4, 8), jnp.int32),
            pltpu.VMEM((1024, 1024), BF16),
            pltpu.VMEM((512, 1024), BF16),
            pltpu.VMEM((1, 128), F32),
            pltpu.VMEM((8, 128), BF16),
            pltpu.VMEM((32, 8, 128), BF16),
            pltpu.VMEM((4, 32, 1024), BF16),
            pltpu.VMEM((32, 8, 128), F32),
            pltpu.VMEM((32, 8, 128), F32),
            pltpu.VMEM((8, 4, 128), F32),
            pltpu.VMEM((8, 4, 128), F32),
            pltpu.VMEM((4, 128), F32),
            pltpu.VMEM((8, 4, 4, 128), F32),
            pltpu.VMEM((32, 4, 128), BF16),
            pltpu.VMEM((32, 4, 128), BF16),
            pltpu.VMEM((4, 128), BF16),
            pltpu.SemaphoreType.DMA((11,)),
            pltpu.SemaphoreType.DMA((7,)),
            pltpu.SemaphoreType.DMA((7,)),
        ],
        compiler_params=pltpu.CompilerParams(collective_id=0, has_side_effects=True),
        name="decoder_layer",
    )(*args, jnp.asarray(rates).reshape(1, 128))


def solution(mesh):
    in_specs = (
        P("req", None, None),
        P("req"),
        P("tp", None),
        P("req", "tp", None),
        P("req", "tp", None),
        P("tp", None),
        P("req", None, None),
        P("req", None, None),
        P("tp", None, None),
        P("tp", None, None),
    )
    out_specs = P("req", None, None)
    return jax.shard_map(
        per_device, mesh=mesh, in_specs=in_specs, out_specs=out_specs, check_vma=False
    )
```

```python
import functools

import jax
import jax.numpy as jnp
import numpy as np
from jax import lax
from jax.experimental import pallas as pl
from jax.experimental.pallas import tpu as pltpu
from jax.sharding import PartitionSpec as P

EPSILON = 1e-05
ROPE_BASE = 10000.0
NEGATIVE = -1e30
MESH = pl.DeviceIdType.MESH
F32 = jnp.float32
BF16 = jnp.bfloat16


def hops(offset):
    return min(offset, 4 - offset)


PEERS = sorted(
    [(dx, dz, dc) for dx in range(4) for dz in range(4) for dc in range(2) if dx or dz or dc],
    key=lambda o: -(hops(o[0]) + hops(o[1]) + 0.5 * o[2]),
)


def stack_rows(pieces):
    return jnp.concatenate(pieces, axis=0)


def kernel(
    hidden_h, lengths_h, qkv_h, keys_h, values_h, outw_h, ids_h, comb_h, gate_h, down_h, rates_h,
    out_h,
    hidden_v, lengths_s, qkv_v, keys_v, values_v, ids_v, comb_v, gate_v, down_v, rates_v,
    qsend, qbuf, wbuf, asend, abuf, pick, rsend, rbuf, kept, ysend, ypair, hsend, hbuf,
    lsem, ssem, rsem,
):
    me = lax.axis_index("tp")
    x = lax.div(me, 8)
    z = lax.rem(lax.div(me, 2), 4)
    c = lax.rem(me, 2)

    def device(offset):
        dx, dz, dc = offset
        px = lax.rem(x + dx, 4) if dx else x
        pz = lax.rem(z + dz, 4) if dz else z
        pc = lax.rem(c + dc, 2) if dc else c
        return px, pz, pc

    def index(offset):
        px, pz, pc = device(offset)
        return px * 8 + pz * 2 + pc

    peers = [index(o) for o in PEERS]

    barrier = pltpu.get_barrier_semaphore()
    for p in peers:
        pl.semaphore_signal(barrier, inc=1, device_id={"tp": p}, device_id_type=MESH)

    def load(src, dst, i):
        copy = pltpu.make_async_copy(src, dst, lsem.at[i])
        copy.start()
        return copy

    c_hidden = load(hidden_h, hidden_v, 0)
    c_len = load(lengths_h, lengths_s, 1)
    c_qkv0 = load(qkv_h, qkv_v.at[pl.ds(0, 64)], 2)
    c_qkv1 = load(qkv_h, qkv_v.at[pl.ds(64, 64)], 3)
    c_rates = load(rates_h, rates_v, 4)
    c_keys = load(keys_h, keys_v, 5)
    c_values = load(values_h, values_v, 6)
    c_ids = load(ids_h, ids_v, 7)
    c_comb = load(comb_h, comb_v, 8)
    c_gate = load(gate_h.at[0], gate_v, 9)
    c_down = load(down_h.at[0], down_v, 10)

    def send(src, dst, phase, p):
        pltpu.make_async_remote_copy(
            src_ref=src, dst_ref=dst, send_sem=ssem.at[phase], recv_sem=rsem.at[phase],
            device_id={"tp": p}, device_id_type=MESH,
        ).start()

    def wait_bytes(ref, sem):
        pltpu.make_async_copy(ref, ref, sem).wait()

    sub = lax.broadcasted_iota(jnp.int32, (8, 128), 0)
    lane = lax.broadcasted_iota(jnp.int32, (8, 128), 1)
    low_half = lane < 64
    top_rows = sub < 4

    c_hidden.wait()
    rows = stack_rows([hidden_v[r].astype(F32) for r in range(4)])
    normed = (
        rows * lax.rsqrt(jnp.mean(rows * rows, axis=-1, keepdims=True) + EPSILON)
    ).astype(BF16)
    c_len.wait()
    lens = [lengths_s[r] for r in range(4)]
    c_rates.wait()
    front = jnp.where(top_rows, lens[0], lens[1])
    rear = jnp.where(top_rows, lens[2], lens[3])
    position = (jnp.where(low_half, front, rear) + jnp.bitwise_and(sub, 3)).astype(F32)
    angles = position * jnp.broadcast_to(rates_v[...], (8, 128))
    cosine = jnp.cos(angles)
    sine = jnp.sin(angles)
    c_qkv0.wait()
    c_qkv1.wait()
    head = lax.dot_general(
        normed, qkv_v[...], (((1,), (1,)), ((), ())), preferred_element_type=F32
    )
    head = head.astype(BF16).astype(F32)
    packed = jnp.where(low_half, head[0:8], head[8:16])
    ahead = pltpu.roll(packed, 96, 1)
    behind = pltpu.roll(packed, 32, 1)
    first = jnp.bitwise_and(lane, 63) < 32
    turned = packed * cosine + jnp.where(first, -ahead, behind) * sine
    turned = turned.astype(BF16).astype(F32)
    query = turned * 0.125
    place = jnp.broadcast_to(lax.rem(me, 4), (8, 128))
    query = jnp.where(place >= 2, pltpu.roll(query, 64, 1), query)
    query = jnp.where(jnp.bitwise_and(place, 1) == 1, pltpu.roll(query, 2, 0), query)
    query = jnp.where(place >= 2, pltpu.roll(query, 4, 0), query)
    whole_me = jnp.broadcast_to(me, (8, 128))
    qsend[...] = jnp.where(
        whole_me < 16, query, jnp.where(whole_me < 24, turned, packed)
    ).astype(BF16)
    for k in range(8):
        kept[k // 4, :, (k % 4) * 128 : (k % 4) * 128 + 128] = rows[:, k * 128 : k * 128 + 128]
    target = lax.broadcasted_iota(jnp.int32, (128, 512), 0)
    source = lax.broadcasted_iota(jnp.int32, (128, 512), 1)
    token = 2 * jnp.bitwise_and(lax.shift_right_logical(source, 4), 7) + jnp.bitwise_and(source, 1)
    column = jnp.bitwise_and(lax.shift_right_logical(source, 1), 7)
    pick[...] = jnp.where(target == column * 16 + token, 1.0, 0.0).astype(BF16)

    pl.semaphore_wait(barrier, 31)
    for p in peers:
        send(qsend, qbuf.at[me], 0, p)
    pltpu.make_async_copy(qsend, qbuf.at[me], rsem.at[0]).start()

    for dz in (2, 1, 3):
        send(outw_h, wbuf.at[2 * z + c], 1, x * 8 + lax.rem(z + dz, 4) * 2 + c)
    pltpu.make_async_copy(outw_h, wbuf.at[2 * z + c], rsem.at[1]).start()

    wait_bytes(qbuf, rsem.at[0])
    heads = [qbuf[h].astype(F32) for h in range(16)]
    pair = lax.shift_right_logical(sub, 1)
    mixed = []
    for q in range(4):
        row = []
        for n in range(4):
            tile = heads[4 * n + (3 - q) % 4]
            for p in range(3):
                tile = jnp.where(pair == p, heads[4 * n + (p - q) % 4], tile)
            row.append(tile)
        mixed.append(row)
    rear_head = [jnp.bitwise_and(pair - q, 3) >= 2 for q in range(4)]
    fits = [rear_head[q] != low_half for q in range(4)]
    c_keys.wait()
    c_values.wait()
    zero = jnp.zeros((8, 128), F32)
    cell = lax.broadcasted_iota(jnp.int32, (64, 128), 1) + me * 128
    for r in range(4):
        tiles = []
        for sp in range(2):
            q = 2 * (r % 2) + sp
            row = []
            for n in range(4):
                tile = mixed[q][n] if r < 2 else pltpu.roll(mixed[q][n], 64, 1)
                row.append(jnp.where(fits[q], tile, 0.0))
            tiles.append(row)
        columns = [
            jnp.concatenate(
                [tiles[sp][n] if n == k else zero for n in range(4) for sp in range(2)], axis=0
            )
            for k in range(4)
        ]
        queries = jnp.concatenate(columns, axis=1).astype(BF16)
        scores = lax.dot_general(
            queries, keys_v[r], (((1,), (1,)), ((), ())), preferred_element_type=F32
        )
        live = cell < lens[r]
        masked = jnp.where(live, scores, NEGATIVE)
        peak = jnp.max(masked, axis=-1, keepdims=True)
        weights = jnp.where(live, jnp.exp(masked - peak), 0.0)
        total = jnp.sum(weights, axis=-1, keepdims=True)
        sums = jnp.dot(weights.astype(BF16), values_v[r], preferred_element_type=F32)
        for n in range(4):
            for sp in range(2):
                b = 8 * (2 * n + sp)
                o = sums[b : b + 8, n * 128 : n * 128 + 128]
                o = jnp.where(rear_head[2 * (r % 2) + sp], pltpu.roll(o, 64, 1), o)
                stats = jnp.where(
                    lane < 96,
                    jnp.broadcast_to(peak[b : b + 8], (8, 128)),
                    jnp.broadcast_to(total[b : b + 8], (8, 128)),
                )
                asend[n * 8 + r * 2 + sp] = jnp.where(low_half, o, stats)

    for p in peers:
        send(asend.at[p], abuf.at[me], 2, p)
    pltpu.make_async_copy(asend.at[me], abuf.at[me], rsem.at[2]).start()

    partner = me + 1 - 2 * c
    wait_bytes(wbuf.at[pl.ds(0, 4)], rsem.at[1])
    for k in range(4):
        send(wbuf.at[2 * k + c], wbuf.at[2 * k + c], 3, partner)

    late = jnp.broadcast_to(lax.rem(z, 2), (8, 128)) == 1
    rear_half = jnp.broadcast_to(lax.div(z, 2), (8, 128)) == 1
    q_own = 2 * lax.rem(z, 2) + c
    tile = qbuf[4 * x + lax.rem(7 - q_own, 4)].astype(F32)
    for p in range(3):
        tile = jnp.where(pair == p, qbuf[4 * x + lax.rem(p + 4 - q_own, 4)].astype(F32), tile)
    head_place = jnp.bitwise_and(pair - jnp.broadcast_to(q_own, (8, 128)), 3)
    own_rear = head_place >= 2
    own_queries = jnp.where(
        low_half, jnp.where(own_rear != rear_half, pltpu.roll(tile, 64, 1), tile), 0.0
    )

    def own_rows(i):
        v = qbuf[i].astype(F32)
        v = jnp.where(rear_half, pltpu.roll(v, 64, 1), v)
        return jnp.where(late, pltpu.roll(v, 4, 0), v)

    def per_head(front, rear):
        return [
            jnp.where(
                own_rear,
                jnp.broadcast_to(rear[s : s + 1], (8, 128)),
                jnp.broadcast_to(front[s : s + 1], (8, 128)),
            )
            for s in range(4)
        ]

    new_keys = per_head(own_rows(16 + 2 * x), own_rows(17 + 2 * x))
    new_values = per_head(own_rows(24 + 2 * x), own_rows(25 + 2 * x))
    step = 2 * jnp.broadcast_to(c, (8, 128)) + jnp.bitwise_and(sub, 1)
    new_scores = []
    for s in range(4):
        score = jnp.sum(
            own_queries * new_keys[s], axis=-1, keepdims=True
        )
        new_scores.append(
            jnp.where(step >= s, jnp.broadcast_to(score, (8, 128)), NEGATIVE)
        )
    new_peak = functools.reduce(jnp.maximum, new_scores)
    new_weights = [jnp.exp(v - new_peak) for v in new_scores]
    new_total = functools.reduce(jnp.add, new_weights)
    new_sum = functools.reduce(
        jnp.add,
        [
            new_weights[s].astype(BF16).astype(F32) * new_values[s]
            for s in range(4)
        ],
    )
    c_ids.wait()
    c_comb.wait()
    factors = [
        jnp.sum(
            jnp.where(ids_v[r] == me, comb_v[r], 0).astype(F32), axis=-1, keepdims=True
        )
        * (1.0 / 65536.0)
        for r in range(4)
    ]
    factor = stack_rows(factors)
    wait_bytes(wbuf.at[pl.ds(0, 4)], rsem.at[3])

    wait_bytes(abuf, rsem.at[2])
    peaks = [jnp.broadcast_to(abuf[b][:, 64:65], (8, 128)) for b in range(32)]
    top = functools.reduce(jnp.maximum, peaks + [new_peak])
    total_all = jnp.zeros((8, 128), F32)
    for b in range(32):
        total_all = total_all + jnp.exp(peaks[b] - top) * abuf[b]
    carried = jnp.exp(new_peak - top)
    denominator = jnp.broadcast_to(total_all[:, 96:97], (8, 128)) + carried * new_total
    attended = jnp.where(low_half, (total_all + carried * new_sum) / denominator, 0.0)
    attended = attended + pltpu.roll(attended, 64, 1)
    half = lax.shift_right_logical(lane, 6)
    attended = jnp.concatenate(
        [
            jnp.where(half == head_place, attended, 0.0),
            jnp.where(half + 2 == head_place, attended, 0.0),
        ],
        axis=1,
    ).astype(BF16)
    product = jnp.dot(
        attended, wbuf[...].reshape(256, 1024), preferred_element_type=F32
    )
    product = product + pltpu.roll(product, 4, 0)
    product = product + pltpu.roll(product, 2, 0)
    parts = []
    for m in range(2):
        part = product[:, m * 512 + 384 : m * 512 + 512]
        for k in range(3):
            at = m * 512 + k * 128
            part = jnp.where(pair == k, product[:, at : at + 128], part)
        parts.append(part)
    rsend[...] = jnp.concatenate(parts, axis=0).astype(BF16)
    for p in peers:
        send(rsend, rbuf.at[me], 4, p)
    pltpu.make_async_copy(rsend, rbuf.at[me], rsem.at[4]).start()
    c_gate.wait()
    c_down.wait()
    wait_bytes(rbuf, rsem.at[4])
    projected = jnp.dot(
        pick[...], rbuf[...].reshape(512, 128), preferred_element_type=F32
    )
    rows = []
    for k in range(8):
        at = pl.ds((k % 4) * 128, 128)
        row = kept[k // 4, :, at] + projected[16 * k : 16 * k + 16]
        kept[k // 4, :, at] = row
        rows.append(row)
    rows = jnp.concatenate(rows, axis=1)
    normed = (
        rows * lax.rsqrt(jnp.mean(rows * rows, axis=-1, keepdims=True) + EPSILON)
    ).astype(BF16)
    united = jnp.dot(normed, gate_v[...], preferred_element_type=F32)
    gate = united[:, :512]
    activation = (gate / (1.0 + jnp.exp(-gate)) * united[:, 512:]).astype(BF16)

    def half_outcome(half):
        start = pl.multiple_of(half * 512, 512)
        return factor * jnp.dot(
            activation, down_v[:, pl.ds(start, 512)], preferred_element_type=F32
        )

    ysend[...] = half_outcome(1 - c).astype(BF16)
    send(ysend, ypair, 5, partner)
    mine = half_outcome(c)
    wait_bytes(ypair, rsem.at[5])
    hsend[...] = (mine + ypair[...].astype(F32)).astype(BF16)
    chip = 4 * x + z
    for o in PEERS:
        if o[2] == 0:
            send(hsend, hbuf.at[chip], 6, index(o))
    pltpu.make_async_copy(hsend, hbuf.at[chip], rsem.at[6]).start()
    wait_bytes(hbuf, rsem.at[6])
    final = kept[c]
    for k in range(16):
        final = final + hbuf[k].astype(F32)
    own_half = pl.ds(pl.multiple_of(c * 512, 512), 512)
    for r in range(4):
        out_h[r, :, own_half] = final[4 * r : 4 * r + 4].astype(BF16)
    send(out_h.at[:, :, own_half], out_h.at[:, :, own_half], 7, partner)
    wait_bytes(out_h.at[:, :, pl.ds(pl.multiple_of(512 - c * 512, 512), 512)], rsem.at[7])

    wait_bytes(qbuf.at[pl.ds(0, 31)], ssem.at[0])
    wait_bytes(wbuf.at[pl.ds(0, 3)], ssem.at[1])
    wait_bytes(abuf.at[pl.ds(0, 31)], ssem.at[2])
    wait_bytes(wbuf.at[pl.ds(0, 4)], ssem.at[3])
    wait_bytes(rbuf.at[pl.ds(0, 31)], ssem.at[4])
    wait_bytes(ypair, ssem.at[5])
    wait_bytes(hbuf.at[pl.ds(0, 15)], ssem.at[6])
    wait_bytes(out_h.at[:, :, own_half], ssem.at[7])


def per_device(*args):
    half = np.arange(128) % 32
    rates = (ROPE_BASE ** (-2.0 * half / 64.0)).astype(np.float32)
    anywhere = pl.BlockSpec(memory_space=pl.ANY)
    return pl.pallas_call(
        kernel,
        out_shape=pltpu.VMEM((4, 4, 1024), BF16),
        in_specs=[anywhere] * 11,
        out_specs=pl.BlockSpec(memory_space=pltpu.VMEM),
        scratch_shapes=[
            pltpu.VMEM((4, 4, 1024), BF16),
            pltpu.SMEM((4,), jnp.int32),
            pltpu.VMEM((128, 1024), BF16),
            pltpu.VMEM((4, 128, 512), BF16),
            pltpu.VMEM((4, 128, 512), BF16),
            pltpu.VMEM((4, 4, 8), jnp.int32),
            pltpu.VMEM((4, 4, 8), jnp.int32),
            pltpu.VMEM((1024, 1024), BF16),
            pltpu.VMEM((512, 1024), BF16),
            pltpu.VMEM((1, 128), F32),
            pltpu.VMEM((8, 128), BF16),
            pltpu.VMEM((32, 8, 128), BF16),
            pltpu.VMEM((8, 32, 1024), BF16),
            pltpu.VMEM((32, 8, 128), F32),
            pltpu.VMEM((32, 8, 128), F32),
            pltpu.VMEM((128, 512), BF16),
            pltpu.VMEM((16, 128), BF16),
            pltpu.VMEM((32, 16, 128), BF16),
            pltpu.VMEM((2, 16, 512), F32),
            pltpu.VMEM((16, 512), BF16),
            pltpu.VMEM((16, 512), BF16),
            pltpu.VMEM((16, 512), BF16),
            pltpu.VMEM((16, 16, 512), BF16),
            pltpu.SemaphoreType.DMA((11,)),
            pltpu.SemaphoreType.DMA((8,)),
            pltpu.SemaphoreType.DMA((8,)),
        ],
        compiler_params=pltpu.CompilerParams(collective_id=0, has_side_effects=True),
        name="decoder_layer",
    )(*args, jnp.asarray(rates).reshape(1, 128))


def solution(mesh):
    in_specs = (
        P("req", None, None),
        P("req"),
        P("tp", None),
        P("req", "tp", None),
        P("req", "tp", None),
        P("tp", None),
        P("req", None, None),
        P("req", None, None),
        P("tp", None, None),
        P("tp", None, None),
    )
    out_specs = P("req", None, None)
    return jax.shard_map(
        per_device, mesh=mesh, in_specs=in_specs, out_specs=out_specs, check_vma=False
    )
```

```python
import functools

import jax
import jax.numpy as jnp
import numpy as np
from jax import lax
from jax.experimental import pallas as pl
from jax.experimental.pallas import tpu as pltpu
from jax.sharding import PartitionSpec as P

EPSILON = 1e-05
ROPE_BASE = 10000.0
NEGATIVE = -1e30
MESH = pl.DeviceIdType.MESH
F32 = jnp.float32
BF16 = jnp.bfloat16


def hops(offset):
    return min(offset, 4 - offset)


PEERS = sorted(
    [(dx, dz, dc) for dx in range(4) for dz in range(4) for dc in range(2) if dx or dz or dc],
    key=lambda o: -(hops(o[0]) + hops(o[1]) + 0.5 * o[2]),
)


def stack_rows(pieces):
    return jnp.concatenate(pieces, axis=0)


def kernel(
    hidden_h, lengths_h, qkv_h, keys_h, values_h, outw_h, ids_h, comb_h, gate_h, down_h, rates_h,
    out_h,
    hidden_v, lengths_s, qkv_v, keys_v, values_v, ids_v, comb_v, gate_v, down_v, rates_v,
    qsend, qbuf, wbuf, asend, abuf, pick, rsend, rbuf, kept, hsend, hbuf,
    lsem, ssem, rsem,
):
    me = lax.axis_index("tp")
    x = lax.div(me, 8)
    z = lax.rem(lax.div(me, 2), 4)
    c = lax.rem(me, 2)

    def device(offset):
        dx, dz, dc = offset
        px = lax.rem(x + dx, 4) if dx else x
        pz = lax.rem(z + dz, 4) if dz else z
        pc = lax.rem(c + dc, 2) if dc else c
        return px, pz, pc

    def index(offset):
        px, pz, pc = device(offset)
        return px * 8 + pz * 2 + pc

    peers = [index(o) for o in PEERS]

    partner = me + 1 - 2 * c

    barrier = pltpu.get_barrier_semaphore()
    for p in peers:
        pl.semaphore_signal(barrier, inc=1, device_id={"tp": p}, device_id_type=MESH)

    def load(src, dst, i):
        copy = pltpu.make_async_copy(src, dst, lsem.at[i])
        copy.start()
        return copy

    c_hidden = load(hidden_h, hidden_v, 0)
    c_len = load(lengths_h, lengths_s, 1)
    c_qkv0 = load(qkv_h, qkv_v.at[pl.ds(0, 64)], 2)
    c_qkv1 = load(qkv_h, qkv_v.at[pl.ds(64, 64)], 3)
    c_rates = load(rates_h, rates_v, 4)
    c_keys = load(keys_h, keys_v, 5)
    c_values = load(values_h, values_v, 6)
    c_ids = load(ids_h, ids_v, 7)
    c_comb = load(comb_h, comb_v, 8)
    c_gate = load(gate_h.at[0], gate_v.at[c], 9)
    own_half = pl.ds(pl.multiple_of(c * 512, 512), 512)
    other_half = pl.ds(pl.multiple_of(512 - c * 512, 512), 512)
    c_down = load(down_h.at[0, :, own_half], down_v.at[c], 10)

    def send(src, dst, phase, p):
        pltpu.make_async_remote_copy(
            src_ref=src, dst_ref=dst, send_sem=ssem.at[phase], recv_sem=rsem.at[phase],
            device_id={"tp": p}, device_id_type=MESH,
        ).start()

    def wait_bytes(ref, sem):
        pltpu.make_async_copy(ref, ref, sem).wait()

    sub = lax.broadcasted_iota(jnp.int32, (8, 128), 0)
    lane = lax.broadcasted_iota(jnp.int32, (8, 128), 1)
    low_half = lane < 64
    top_rows = sub < 4

    c_hidden.wait()
    rows = stack_rows([hidden_v[r].astype(F32) for r in range(4)])
    normed = (
        rows * lax.rsqrt(jnp.mean(rows * rows, axis=-1, keepdims=True) + EPSILON)
    ).astype(BF16)
    c_len.wait()
    lens = [lengths_s[r] for r in range(4)]
    c_rates.wait()
    front = jnp.where(top_rows, lens[0], lens[1])
    rear = jnp.where(top_rows, lens[2], lens[3])
    position = (jnp.where(low_half, front, rear) + jnp.bitwise_and(sub, 3)).astype(F32)
    angles = position * jnp.broadcast_to(rates_v[...], (8, 128))
    cosine = jnp.cos(angles)
    sine = jnp.sin(angles)
    c_qkv0.wait()
    c_qkv1.wait()
    head = lax.dot_general(
        normed, qkv_v[...], (((1,), (1,)), ((), ())), preferred_element_type=F32
    )
    head = head.astype(BF16).astype(F32)
    packed = jnp.where(low_half, head[0:8], head[8:16])
    ahead = pltpu.roll(packed, 96, 1)
    behind = pltpu.roll(packed, 32, 1)
    first = jnp.bitwise_and(lane, 63) < 32
    turned = packed * cosine + jnp.where(first, -ahead, behind) * sine
    turned = turned.astype(BF16).astype(F32)
    query = turned * 0.125
    place = jnp.broadcast_to(lax.rem(me, 4), (8, 128))
    query = jnp.where(place >= 2, pltpu.roll(query, 64, 1), query)
    query = jnp.where(jnp.bitwise_and(place, 1) == 1, pltpu.roll(query, 2, 0), query)
    query = jnp.where(place >= 2, pltpu.roll(query, 4, 0), query)
    whole_me = jnp.broadcast_to(me, (8, 128))
    qsend[...] = jnp.where(
        whole_me < 16, query, jnp.where(whole_me < 24, turned, packed)
    ).astype(BF16)
    for k in range(8):
        kept[k // 4, :, (k % 4) * 128 : (k % 4) * 128 + 128] = rows[:, k * 128 : k * 128 + 128]
    target = lax.broadcasted_iota(jnp.int32, (128, 512), 0)
    source = lax.broadcasted_iota(jnp.int32, (128, 512), 1)
    token = 2 * jnp.bitwise_and(lax.shift_right_logical(source, 4), 7) + jnp.bitwise_and(source, 1)
    column = jnp.bitwise_and(lax.shift_right_logical(source, 1), 7)
    pick[...] = jnp.where(target == column * 16 + token, 1.0, 0.0).astype(BF16)

    pl.semaphore_wait(barrier, 31)
    for p in peers:
        send(qsend, qbuf.at[me], 0, p)
    pltpu.make_async_copy(qsend, qbuf.at[me], rsem.at[0]).start()

    for dz in (2, 1, 3):
        send(outw_h, wbuf.at[2 * z + c], 1, x * 8 + lax.rem(z + dz, 4) * 2 + c)
    pltpu.make_async_copy(outw_h, wbuf.at[2 * z + c], rsem.at[1]).start()

    wait_bytes(qbuf, rsem.at[0])
    heads = [qbuf[h].astype(F32) for h in range(16)]
    pair = lax.shift_right_logical(sub, 1)
    mixed = []
    for q in range(4):
        row = []
        for n in range(4):
            tile = heads[4 * n + (3 - q) % 4]
            for p in range(3):
                tile = jnp.where(pair == p, heads[4 * n + (p - q) % 4], tile)
            row.append(tile)
        mixed.append(row)
    rear_head = [jnp.bitwise_and(pair - q, 3) >= 2 for q in range(4)]
    fits = [rear_head[q] != low_half for q in range(4)]
    c_keys.wait()
    c_values.wait()
    zero = jnp.zeros((8, 128), F32)
    all_scores = []
    for r in range(4):
        tiles = []
        for sp in range(2):
            q = 2 * (r % 2) + sp
            row = []
            for n in range(4):
                tile = mixed[q][n] if r < 2 else pltpu.roll(mixed[q][n], 64, 1)
                row.append(jnp.where(fits[q], tile, 0.0))
            tiles.append(row)
        columns = [
            jnp.concatenate(
                [tiles[sp][n] if n == k else zero for n in range(4) for sp in range(2)], axis=0
            )
            for k in range(4)
        ]
        queries = jnp.concatenate(columns, axis=1).astype(BF16)
        all_scores.append(
            lax.dot_general(
                queries, keys_v[r], (((1,), (1,)), ((), ())), preferred_element_type=F32
            )
        )
    cell = lax.broadcasted_iota(jnp.int32, (64, 128), 1) + me * 128
    live = [cell < lens[r] for r in range(4)]
    masked = [jnp.where(live[r], all_scores[r], NEGATIVE) for r in range(4)]
    peaks = [jnp.max(masked[r], axis=-1, keepdims=True) for r in range(4)]
    weights = [jnp.where(live[r], jnp.exp(masked[r] - peaks[r]), 0.0) for r in range(4)]
    sums = [
        jnp.dot(weights[r].astype(BF16), values_v[r], preferred_element_type=F32)
        for r in range(4)
    ]
    totals = [jnp.sum(weights[r], axis=-1, keepdims=True) for r in range(4)]
    for r in range(4):
        stats = jnp.where(
            lax.broadcasted_iota(jnp.int32, (64, 128), 1) < 96, peaks[r], totals[r]
        )
        for n in range(4):
            for sp in range(2):
                b = 8 * (2 * n + sp)
                o = sums[r][b : b + 8, n * 128 : n * 128 + 128]
                o = jnp.where(rear_head[2 * (r % 2) + sp], pltpu.roll(o, 64, 1), o)
                asend[n * 8 + r * 2 + sp] = jnp.where(low_half, o, stats[b : b + 8])

    for p in peers:
        send(asend.at[p], abuf.at[me], 2, p)
    pltpu.make_async_copy(asend.at[me], abuf.at[me], rsem.at[2]).start()

    wait_bytes(wbuf.at[pl.ds(0, 4)], rsem.at[1])
    for k in range(4):
        send(wbuf.at[2 * k + c], wbuf.at[2 * k + c], 3, partner)

    send(gate_h.at[0], gate_v.at[c], 5, partner)
    send(down_h.at[0, :, other_half], down_v.at[c], 8, partner)

    late = jnp.broadcast_to(lax.rem(z, 2), (8, 128)) == 1
    rear_half = jnp.broadcast_to(lax.div(z, 2), (8, 128)) == 1
    q_own = 2 * lax.rem(z, 2) + c
    tile = qbuf[4 * x + lax.rem(7 - q_own, 4)].astype(F32)
    for p in range(3):
        tile = jnp.where(pair == p, qbuf[4 * x + lax.rem(p + 4 - q_own, 4)].astype(F32), tile)
    head_place = jnp.bitwise_and(pair - jnp.broadcast_to(q_own, (8, 128)), 3)
    own_rear = head_place >= 2
    own_queries = jnp.where(
        low_half, jnp.where(own_rear != rear_half, pltpu.roll(tile, 64, 1), tile), 0.0
    )

    def own_rows(i):
        v = qbuf[i].astype(F32)
        v = jnp.where(rear_half, pltpu.roll(v, 64, 1), v)
        return jnp.where(late, pltpu.roll(v, 4, 0), v)

    def per_head(front, rear):
        return [
            jnp.where(
                own_rear,
                jnp.broadcast_to(rear[s : s + 1], (8, 128)),
                jnp.broadcast_to(front[s : s + 1], (8, 128)),
            )
            for s in range(4)
        ]

    new_keys = per_head(own_rows(16 + 2 * x), own_rows(17 + 2 * x))
    new_values = per_head(own_rows(24 + 2 * x), own_rows(25 + 2 * x))
    step = 2 * jnp.broadcast_to(c, (8, 128)) + jnp.bitwise_and(sub, 1)
    new_scores = []
    for s in range(4):
        score = jnp.sum(
            own_queries * new_keys[s], axis=-1, keepdims=True
        )
        new_scores.append(
            jnp.where(step >= s, jnp.broadcast_to(score, (8, 128)), NEGATIVE)
        )
    new_peak = functools.reduce(jnp.maximum, new_scores)
    new_weights = [jnp.exp(v - new_peak) for v in new_scores]
    new_total = functools.reduce(jnp.add, new_weights)
    new_sum = functools.reduce(
        jnp.add,
        [
            new_weights[s].astype(BF16).astype(F32) * new_values[s]
            for s in range(4)
        ],
    )
    c_ids.wait()
    c_comb.wait()
    factors = [
        stack_rows(
            [
                jnp.sum(
                    jnp.where(ids_v[r] == me - c + e, comb_v[r], 0).astype(F32),
                    axis=-1,
                    keepdims=True,
                )
                for r in range(4)
            ]
        )
        * (1.0 / 65536.0)
        for e in range(2)
    ]
    wait_bytes(wbuf.at[pl.ds(0, 4)], rsem.at[3])

    wait_bytes(abuf, rsem.at[2])
    peaks = [jnp.broadcast_to(abuf[b][:, 64:65], (8, 128)) for b in range(32)]
    top = functools.reduce(jnp.maximum, peaks + [new_peak])
    total_all = jnp.zeros((8, 128), F32)
    for b in range(32):
        total_all = total_all + jnp.exp(peaks[b] - top) * abuf[b]
    carried = jnp.exp(new_peak - top)
    denominator = jnp.broadcast_to(total_all[:, 96:97], (8, 128)) + carried * new_total
    attended = jnp.where(low_half, (total_all + carried * new_sum) / denominator, 0.0)
    attended = attended + pltpu.roll(attended, 64, 1)
    half = lax.shift_right_logical(lane, 6)
    attended = jnp.concatenate(
        [
            jnp.where(half == head_place, attended, 0.0),
            jnp.where(half + 2 == head_place, attended, 0.0),
        ],
        axis=1,
    ).astype(BF16)
    product = jnp.dot(
        attended, wbuf[...].reshape(256, 1024), preferred_element_type=F32
    )
    product = product + pltpu.roll(product, 4, 0)
    product = product + pltpu.roll(product, 2, 0)
    parts = []
    for m in range(2):
        part = product[:, m * 512 + 384 : m * 512 + 512]
        for k in range(3):
            at = m * 512 + k * 128
            part = jnp.where(pair == k, product[:, at : at + 128], part)
        parts.append(part)
    rsend[...] = jnp.concatenate(parts, axis=0).astype(BF16)
    for p in peers:
        send(rsend, rbuf.at[me], 4, p)
    pltpu.make_async_copy(rsend, rbuf.at[me], rsem.at[4]).start()
    c_gate.wait()
    c_down.wait()
    wait_bytes(rbuf, rsem.at[4])
    projected = jnp.dot(
        pick[...], rbuf[...].reshape(512, 128), preferred_element_type=F32
    )
    rows = []
    for k in range(8):
        at = pl.ds((k % 4) * 128, 128)
        row = kept[k // 4, :, at] + projected[16 * k : 16 * k + 16]
        kept[k // 4, :, at] = row
        rows.append(row)
    rows = jnp.concatenate(rows, axis=1)
    normed = (
        rows * lax.rsqrt(jnp.mean(rows * rows, axis=-1, keepdims=True) + EPSILON)
    ).astype(BF16)
    wait_bytes(gate_v.at[0], rsem.at[5])
    wait_bytes(down_v.at[0], rsem.at[8])
    activations = []
    for e in range(2):
        united = jnp.dot(normed, gate_v[e], preferred_element_type=F32)
        gate = united[:, :512]
        activations.append(
            (gate / (1.0 + jnp.exp(-gate)) * united[:, 512:] * factors[e]).astype(BF16)
        )
    hsend[...] = jnp.dot(
        jnp.concatenate(activations, axis=1),
        down_v[...].reshape(1024, 512),
        preferred_element_type=F32,
    ).astype(BF16)
    chip = 4 * x + z
    for o in PEERS:
        if o[2] == 0:
            send(hsend, hbuf.at[chip], 6, index(o))
    pltpu.make_async_copy(hsend, hbuf.at[chip], rsem.at[6]).start()
    wait_bytes(hbuf, rsem.at[6])
    final = kept[c]
    for k in range(16):
        final = final + hbuf[k].astype(F32)
    for r in range(4):
        out_h[r, :, own_half] = final[4 * r : 4 * r + 4].astype(BF16)
    send(out_h.at[:, :, own_half], out_h.at[:, :, own_half], 7, partner)
    wait_bytes(out_h.at[:, :, other_half], rsem.at[7])

    wait_bytes(qbuf.at[pl.ds(0, 31)], ssem.at[0])
    wait_bytes(wbuf.at[pl.ds(0, 3)], ssem.at[1])
    wait_bytes(abuf.at[pl.ds(0, 31)], ssem.at[2])
    wait_bytes(wbuf.at[pl.ds(0, 4)], ssem.at[3])
    wait_bytes(rbuf.at[pl.ds(0, 31)], ssem.at[4])
    wait_bytes(gate_v.at[0], ssem.at[5])
    wait_bytes(down_v.at[0], ssem.at[8])
    wait_bytes(hbuf.at[pl.ds(0, 15)], ssem.at[6])
    wait_bytes(out_h.at[:, :, own_half], ssem.at[7])


def per_device(*args):
    half = np.arange(128) % 32
    rates = (ROPE_BASE ** (-2.0 * half / 64.0)).astype(np.float32)
    anywhere = pl.BlockSpec(memory_space=pl.ANY)
    return pl.pallas_call(
        kernel,
        out_shape=pltpu.VMEM((4, 4, 1024), BF16),
        in_specs=[anywhere] * 11,
        out_specs=pl.BlockSpec(memory_space=pltpu.VMEM),
        scratch_shapes=[
            pltpu.VMEM((4, 4, 1024), BF16),
            pltpu.SMEM((4,), jnp.int32),
            pltpu.VMEM((128, 1024), BF16),
            pltpu.VMEM((4, 128, 512), BF16),
            pltpu.VMEM((4, 128, 512), BF16),
            pltpu.VMEM((4, 4, 8), jnp.int32),
            pltpu.VMEM((4, 4, 8), jnp.int32),
            pltpu.VMEM((2, 1024, 1024), BF16),
            pltpu.VMEM((2, 512, 512), BF16),
            pltpu.VMEM((1, 128), F32),
            pltpu.VMEM((8, 128), BF16),
            pltpu.VMEM((32, 8, 128), BF16),
            pltpu.VMEM((8, 32, 1024), BF16),
            pltpu.VMEM((32, 8, 128), F32),
            pltpu.VMEM((32, 8, 128), F32),
            pltpu.VMEM((128, 512), BF16),
            pltpu.VMEM((16, 128), BF16),
            pltpu.VMEM((32, 16, 128), BF16),
            pltpu.VMEM((2, 16, 512), F32),
            pltpu.VMEM((16, 512), BF16),
            pltpu.VMEM((16, 16, 512), BF16),
            pltpu.SemaphoreType.DMA((11,)),
            pltpu.SemaphoreType.DMA((9,)),
            pltpu.SemaphoreType.DMA((9,)),
        ],
        compiler_params=pltpu.CompilerParams(collective_id=0, has_side_effects=True),
        name="decoder_layer",
    )(*args, jnp.asarray(rates).reshape(1, 128))


def solution(mesh):
    in_specs = (
        P("req", None, None),
        P("req"),
        P("tp", None),
        P("req", "tp", None),
        P("req", "tp", None),
        P("tp", None),
        P("req", None, None),
        P("req", None, None),
        P("tp", None, None),
        P("tp", None, None),
    )
    out_specs = P("req", None, None)
    return jax.shard_map(
        per_device, mesh=mesh, in_specs=in_specs, out_specs=out_specs, check_vma=False
    )
```

```python
import functools

import jax
import jax.numpy as jnp
import numpy as np
from jax import lax
from jax.experimental import pallas as pl
from jax.experimental.pallas import tpu as pltpu
from jax.sharding import PartitionSpec as P

EPSILON = 1e-05
ROPE_BASE = 10000.0
NEGATIVE = -1e30
MESH = pl.DeviceIdType.MESH
F32 = jnp.float32
BF16 = jnp.bfloat16


def hops(offset):
    return min(offset, 4 - offset)


PEERS = sorted(
    [(dx, dz, dc) for dx in range(4) for dz in range(4) for dc in range(2) if dx or dz or dc],
    key=lambda o: -(hops(o[0]) + hops(o[1]) + 0.5 * o[2]),
)


def tree(op, items):
    while len(items) > 1:
        items = [
            op(items[k], items[k + 1]) if k + 1 < len(items) else items[k]
            for k in range(0, len(items), 2)
        ]
    return items[0]


def stack_rows(pieces):
    return jnp.concatenate(pieces, axis=0)


def kernel(
    hidden_h, lengths_h, qkv_h, keys_h, values_h, outw_h, ids_h, comb_h, gate_h, down_h, rates_h,
    out_h,
    hidden_v, lengths_s, qkv_v, keys_v, values_v, ids_v, comb_v, gate_v, down_v, rates_v,
    qsend, qbuf, wbuf, asend, abuf, pick, rsend, rbuf, kept, hsend, hbuf,
    lsem, ssem, rsem,
):
    me = lax.axis_index("tp")
    x = lax.div(me, 8)
    z = lax.rem(lax.div(me, 2), 4)
    c = lax.rem(me, 2)

    def device(offset):
        dx, dz, dc = offset
        px = lax.rem(x + dx, 4) if dx else x
        pz = lax.rem(z + dz, 4) if dz else z
        pc = lax.rem(c + dc, 2) if dc else c
        return px, pz, pc

    def index(offset):
        px, pz, pc = device(offset)
        return px * 8 + pz * 2 + pc

    peers = [index(o) for o in PEERS]

    partner = me + 1 - 2 * c

    barrier = pltpu.get_barrier_semaphore()
    for p in peers:
        pl.semaphore_signal(barrier, inc=1, device_id={"tp": p}, device_id_type=MESH)

    def load(src, dst, i):
        copy = pltpu.make_async_copy(src, dst, lsem.at[i])
        copy.start()
        return copy

    c_hidden = load(hidden_h, hidden_v, 0)
    c_len = load(lengths_h, lengths_s, 1)
    c_qkv0 = load(qkv_h, qkv_v.at[pl.ds(0, 64)], 2)
    c_qkv1 = load(qkv_h, qkv_v.at[pl.ds(64, 64)], 3)
    c_rates = load(rates_h, rates_v, 4)
    c_keys = load(keys_h, keys_v, 5)
    c_values = load(values_h, values_v, 6)
    c_ids = load(ids_h, ids_v, 7)
    c_comb = load(comb_h, comb_v, 8)
    c_gate = load(gate_h.at[0], gate_v.at[c], 9)
    own_half = pl.ds(pl.multiple_of(c * 512, 512), 512)
    other_half = pl.ds(pl.multiple_of(512 - c * 512, 512), 512)
    c_down = load(down_h.at[0, :, other_half], down_v.at[c], 10)

    def send(src, dst, phase, p):
        pltpu.make_async_remote_copy(
            src_ref=src, dst_ref=dst, send_sem=ssem.at[phase], recv_sem=rsem.at[phase],
            device_id={"tp": p}, device_id_type=MESH,
        ).start()

    def wait_bytes(ref, sem):
        pltpu.make_async_copy(ref, ref, sem).wait()

    sub = lax.broadcasted_iota(jnp.int32, (8, 128), 0)
    lane = lax.broadcasted_iota(jnp.int32, (8, 128), 1)
    low_half = lane < 64
    top_rows = sub < 4

    c_hidden.wait()
    rows = stack_rows([hidden_v[r].astype(F32) for r in range(4)])
    normed = (
        rows * lax.rsqrt(jnp.mean(rows * rows, axis=-1, keepdims=True) + EPSILON)
    ).astype(BF16)
    c_len.wait()
    lens = [lengths_s[r] for r in range(4)]
    c_rates.wait()
    front = jnp.where(top_rows, lens[0], lens[1])
    rear = jnp.where(top_rows, lens[2], lens[3])
    position = (jnp.where(low_half, front, rear) + jnp.bitwise_and(sub, 3)).astype(F32)
    angles = position * jnp.broadcast_to(rates_v[...], (8, 128))
    cosine = jnp.cos(angles)
    sine = jnp.sin(angles)
    c_qkv0.wait()
    c_qkv1.wait()
    head = lax.dot_general(
        normed, qkv_v[...], (((1,), (1,)), ((), ())), preferred_element_type=F32
    )
    head = head.astype(BF16).astype(F32)
    packed = jnp.where(low_half, head[0:8], head[8:16])
    ahead = pltpu.roll(packed, 96, 1)
    behind = pltpu.roll(packed, 32, 1)
    first = jnp.bitwise_and(lane, 63) < 32
    turned = packed * cosine + jnp.where(first, -ahead, behind) * sine
    turned = turned.astype(BF16).astype(F32)
    query = turned * 0.125
    place = jnp.broadcast_to(lax.rem(me, 4), (8, 128))
    query = jnp.where(place >= 2, pltpu.roll(query, 64, 1), query)
    query = jnp.where(jnp.bitwise_and(place, 1) == 1, pltpu.roll(query, 2, 0), query)
    query = jnp.where(place >= 2, pltpu.roll(query, 4, 0), query)
    whole_me = jnp.broadcast_to(me, (8, 128))
    qsend[...] = jnp.where(
        whole_me < 16, query, jnp.where(whole_me < 24, turned, packed)
    ).astype(BF16)
    for k in range(8):
        kept[k // 4, :, (k % 4) * 128 : (k % 4) * 128 + 128] = rows[:, k * 128 : k * 128 + 128]
    target = lax.broadcasted_iota(jnp.int32, (128, 512), 0)
    source = lax.broadcasted_iota(jnp.int32, (128, 512), 1)
    token = 2 * jnp.bitwise_and(lax.shift_right_logical(source, 4), 7) + jnp.bitwise_and(source, 1)
    column = jnp.bitwise_and(lax.shift_right_logical(source, 1), 7)
    pick[...] = jnp.where(target == column * 16 + token, 1.0, 0.0).astype(BF16)

    pl.semaphore_wait(barrier, 31)
    for p in peers:
        send(qsend, qbuf.at[me], 0, p)
    pltpu.make_async_copy(qsend, qbuf.at[me], rsem.at[0]).start()

    for dz in (2, 1, 3):
        send(outw_h, wbuf.at[2 * z + c], 1, x * 8 + lax.rem(z + dz, 4) * 2 + c)
    pltpu.make_async_copy(outw_h, wbuf.at[2 * z + c], rsem.at[1]).start()

    wait_bytes(qbuf, rsem.at[0])
    heads = [qbuf[h].astype(F32) for h in range(16)]
    pair = lax.shift_right_logical(sub, 1)
    mixed = []
    for q in range(4):
        row = []
        for n in range(4):
            tile = heads[4 * n + (3 - q) % 4]
            for p in range(3):
                tile = jnp.where(pair == p, heads[4 * n + (p - q) % 4], tile)
            row.append(tile)
        mixed.append(row)
    rear_head = [jnp.bitwise_and(pair - q, 3) >= 2 for q in range(4)]
    fits = [rear_head[q] != low_half for q in range(4)]
    c_keys.wait()
    c_values.wait()
    zero = jnp.zeros((8, 128), F32)
    all_scores = []
    for r in range(4):
        tiles = []
        for sp in range(2):
            q = 2 * (r % 2) + sp
            row = []
            for n in range(4):
                tile = mixed[q][n] if r < 2 else pltpu.roll(mixed[q][n], 64, 1)
                row.append(jnp.where(fits[q], tile, 0.0))
            tiles.append(row)
        columns = [
            jnp.concatenate(
                [tiles[sp][n] if n == k else zero for n in range(4) for sp in range(2)], axis=0
            )
            for k in range(4)
        ]
        queries = jnp.concatenate(columns, axis=1).astype(BF16)
        all_scores.append(
            lax.dot_general(
                queries, keys_v[r], (((1,), (1,)), ((), ())), preferred_element_type=F32
            )
        )
    cell = lax.broadcasted_iota(jnp.int32, (64, 128), 1) + me * 128
    live = [cell < lens[r] for r in range(4)]
    masked = [jnp.where(live[r], all_scores[r], NEGATIVE) for r in range(4)]
    peaks = [jnp.max(masked[r], axis=-1, keepdims=True) for r in range(4)]
    weights = [jnp.where(live[r], jnp.exp(masked[r] - peaks[r]), 0.0) for r in range(4)]
    sums = [
        jnp.dot(weights[r].astype(BF16), values_v[r], preferred_element_type=F32)
        for r in range(4)
    ]
    totals = [jnp.sum(weights[r], axis=-1, keepdims=True) for r in range(4)]
    for r in range(4):
        stats = jnp.where(
            lax.broadcasted_iota(jnp.int32, (64, 128), 1) < 96, peaks[r], totals[r]
        )
        for n in range(4):
            for sp in range(2):
                b = 8 * (2 * n + sp)
                o = sums[r][b : b + 8, n * 128 : n * 128 + 128]
                o = jnp.where(rear_head[2 * (r % 2) + sp], pltpu.roll(o, 64, 1), o)
                asend[n * 8 + r * 2 + sp] = jnp.where(low_half, o, stats[b : b + 8])

    for p in peers:
        send(asend.at[p], abuf.at[me], 2, p)
    pltpu.make_async_copy(asend.at[me], abuf.at[me], rsem.at[2]).start()

    wait_bytes(wbuf.at[pl.ds(0, 4)], rsem.at[1])
    for k in range(4):
        send(wbuf.at[2 * k + c], wbuf.at[2 * k + c], 3, partner)

    send(gate_h.at[0], gate_v.at[c], 5, partner)
    send(down_h.at[0, :, own_half], down_v.at[c], 8, partner)

    late = jnp.broadcast_to(lax.rem(z, 2), (8, 128)) == 1
    rear_half = jnp.broadcast_to(lax.div(z, 2), (8, 128)) == 1
    q_own = 2 * lax.rem(z, 2) + c
    tile = qbuf[4 * x + lax.rem(7 - q_own, 4)].astype(F32)
    for p in range(3):
        tile = jnp.where(pair == p, qbuf[4 * x + lax.rem(p + 4 - q_own, 4)].astype(F32), tile)
    head_place = jnp.bitwise_and(pair - jnp.broadcast_to(q_own, (8, 128)), 3)
    own_rear = head_place >= 2
    own_queries = jnp.where(
        low_half, jnp.where(own_rear != rear_half, pltpu.roll(tile, 64, 1), tile), 0.0
    )

    def own_rows(i):
        v = qbuf[i].astype(F32)
        v = jnp.where(rear_half, pltpu.roll(v, 64, 1), v)
        return jnp.where(late, pltpu.roll(v, 4, 0), v)

    def per_head(front, rear):
        return [
            jnp.where(
                own_rear,
                jnp.broadcast_to(rear[s : s + 1], (8, 128)),
                jnp.broadcast_to(front[s : s + 1], (8, 128)),
            )
            for s in range(4)
        ]

    new_keys = per_head(own_rows(16 + 2 * x), own_rows(17 + 2 * x))
    new_values = per_head(own_rows(24 + 2 * x), own_rows(25 + 2 * x))
    step = 2 * jnp.broadcast_to(c, (8, 128)) + jnp.bitwise_and(sub, 1)
    new_scores = []
    for s in range(4):
        score = jnp.sum(
            own_queries * new_keys[s], axis=-1, keepdims=True
        )
        new_scores.append(
            jnp.where(step >= s, jnp.broadcast_to(score, (8, 128)), NEGATIVE)
        )
    new_peak = functools.reduce(jnp.maximum, new_scores)
    new_weights = [jnp.exp(v - new_peak) for v in new_scores]
    new_total = functools.reduce(jnp.add, new_weights)
    new_sum = functools.reduce(
        jnp.add,
        [
            new_weights[s].astype(BF16).astype(F32) * new_values[s]
            for s in range(4)
        ],
    )
    c_ids.wait()
    c_comb.wait()
    factors = [
        stack_rows(
            [
                jnp.sum(
                    jnp.where(ids_v[r] == me - c + e, comb_v[r], 0).astype(F32),
                    axis=-1,
                    keepdims=True,
                )
                for r in range(4)
            ]
        )
        * (1.0 / 65536.0)
        for e in range(2)
    ]
    wait_bytes(wbuf.at[pl.ds(0, 4)], rsem.at[3])

    wait_bytes(abuf, rsem.at[2])
    peaks = [jnp.broadcast_to(abuf[b][:, 64:65], (8, 128)) for b in range(32)]
    top = tree(jnp.maximum, peaks + [new_peak])
    total_all = tree(jnp.add, [jnp.exp(peaks[b] - top) * abuf[b] for b in range(32)])
    carried = jnp.exp(new_peak - top)
    denominator = jnp.broadcast_to(total_all[:, 96:97], (8, 128)) + carried * new_total
    attended = jnp.where(low_half, (total_all + carried * new_sum) / denominator, 0.0)
    attended = attended + pltpu.roll(attended, 64, 1)
    half = lax.shift_right_logical(lane, 6)
    attended = jnp.concatenate(
        [
            jnp.where(half == head_place, attended, 0.0),
            jnp.where(half + 2 == head_place, attended, 0.0),
        ],
        axis=1,
    ).astype(BF16)
    product = jnp.dot(
        attended, wbuf[...].reshape(256, 1024), preferred_element_type=F32
    )
    product = product + pltpu.roll(product, 4, 0)
    product = product + pltpu.roll(product, 2, 0)
    parts = []
    for m in range(2):
        part = product[:, m * 512 + 384 : m * 512 + 512]
        for k in range(3):
            at = m * 512 + k * 128
            part = jnp.where(pair == k, product[:, at : at + 128], part)
        parts.append(part)
    rsend[...] = jnp.concatenate(parts, axis=0).astype(BF16)
    for p in peers:
        send(rsend, rbuf.at[me], 4, p)
    pltpu.make_async_copy(rsend, rbuf.at[me], rsem.at[4]).start()
    c_gate.wait()
    c_down.wait()
    wait_bytes(rbuf, rsem.at[4])
    projected = jnp.dot(
        pick[...], rbuf[...].reshape(512, 128), preferred_element_type=F32
    )
    rows = []
    for k in range(8):
        at = pl.ds((k % 4) * 128, 128)
        row = kept[k // 4, :, at] + projected[16 * k : 16 * k + 16]
        kept[k // 4, :, at] = row
        rows.append(row)
    rows = jnp.concatenate(rows, axis=1)
    normed = (
        rows * lax.rsqrt(jnp.mean(rows * rows, axis=-1, keepdims=True) + EPSILON)
    ).astype(BF16)
    wait_bytes(gate_v.at[0], rsem.at[5])
    wait_bytes(down_v.at[0], rsem.at[8])
    activations = []
    for e in range(2):
        united = jnp.dot(normed, gate_v[e], preferred_element_type=F32)
        gate = united[:, :512]
        activations.append(
            (gate / (1.0 + jnp.exp(-gate)) * united[:, 512:] * factors[e]).astype(BF16)
        )
    hsend[...] = jnp.dot(
        jnp.concatenate(activations, axis=1),
        down_v[...].reshape(1024, 512),
        preferred_element_type=F32,
    ).astype(BF16)
    chip = 4 * x + z
    for o in PEERS:
        if o[2] == 1:
            send(hsend, hbuf.at[chip], 6, index(o))
    wait_bytes(hbuf, rsem.at[6])
    final = kept[c] + tree(jnp.add, [hbuf[k].astype(F32) for k in range(16)])
    for r in range(4):
        out_h[r, :, own_half] = final[4 * r : 4 * r + 4].astype(BF16)
    send(out_h.at[:, :, own_half], out_h.at[:, :, own_half], 7, partner)
    wait_bytes(out_h.at[:, :, other_half], rsem.at[7])

    wait_bytes(qbuf.at[pl.ds(0, 31)], ssem.at[0])
    wait_bytes(wbuf.at[pl.ds(0, 3)], ssem.at[1])
    wait_bytes(abuf.at[pl.ds(0, 31)], ssem.at[2])
    wait_bytes(wbuf.at[pl.ds(0, 4)], ssem.at[3])
    wait_bytes(rbuf.at[pl.ds(0, 31)], ssem.at[4])
    wait_bytes(gate_v.at[0], ssem.at[5])
    wait_bytes(down_v.at[0], ssem.at[8])
    wait_bytes(hbuf, ssem.at[6])
    wait_bytes(out_h.at[:, :, own_half], ssem.at[7])


def per_device(*args):
    half = np.arange(128) % 32
    rates = (ROPE_BASE ** (-2.0 * half / 64.0)).astype(np.float32)
    anywhere = pl.BlockSpec(memory_space=pl.ANY)
    return pl.pallas_call(
        kernel,
        out_shape=pltpu.VMEM((4, 4, 1024), BF16),
        in_specs=[anywhere] * 11,
        out_specs=pl.BlockSpec(memory_space=pltpu.VMEM),
        scratch_shapes=[
            pltpu.VMEM((4, 4, 1024), BF16),
            pltpu.SMEM((4,), jnp.int32),
            pltpu.VMEM((128, 1024), BF16),
            pltpu.VMEM((4, 128, 512), BF16),
            pltpu.VMEM((4, 128, 512), BF16),
            pltpu.VMEM((4, 4, 8), jnp.int32),
            pltpu.VMEM((4, 4, 8), jnp.int32),
            pltpu.VMEM((2, 1024, 1024), BF16),
            pltpu.VMEM((2, 512, 512), BF16),
            pltpu.VMEM((1, 128), F32),
            pltpu.VMEM((8, 128), BF16),
            pltpu.VMEM((32, 8, 128), BF16),
            pltpu.VMEM((8, 32, 1024), BF16),
            pltpu.VMEM((32, 8, 128), F32),
            pltpu.VMEM((32, 8, 128), F32),
            pltpu.VMEM((128, 512), BF16),
            pltpu.VMEM((16, 128), BF16),
            pltpu.VMEM((32, 16, 128), BF16),
            pltpu.VMEM((2, 16, 512), F32),
            pltpu.VMEM((16, 512), BF16),
            pltpu.VMEM((16, 16, 512), BF16),
            pltpu.SemaphoreType.DMA((11,)),
            pltpu.SemaphoreType.DMA((9,)),
            pltpu.SemaphoreType.DMA((9,)),
        ],
        compiler_params=pltpu.CompilerParams(collective_id=0, has_side_effects=True),
        name="decoder_layer",
    )(*args, jnp.asarray(rates).reshape(1, 128))


def solution(mesh):
    in_specs = (
        P("req", None, None),
        P("req"),
        P("tp", None),
        P("req", "tp", None),
        P("req", "tp", None),
        P("tp", None),
        P("req", None, None),
        P("req", None, None),
        P("tp", None, None),
        P("tp", None, None),
    )
    out_specs = P("req", None, None)
    return jax.shard_map(
        per_device, mesh=mesh, in_specs=in_specs, out_specs=out_specs, check_vma=False
    )
```

```python
import functools

import jax
import jax.numpy as jnp
import numpy as np
from jax import lax
from jax.experimental import pallas as pl
from jax.experimental.pallas import tpu as pltpu
from jax.sharding import PartitionSpec as P

EPSILON = 1e-05
ROPE_BASE = 10000.0
NEGATIVE = -1e30
MESH = pl.DeviceIdType.MESH
F32 = jnp.float32
BF16 = jnp.bfloat16


def hops(offset):
    return min(offset, 4 - offset)


PEERS = sorted(
    [(dx, dz, dc) for dx in range(4) for dz in range(4) for dc in range(2) if dx or dz or dc],
    key=lambda o: -(hops(o[0]) + hops(o[1]) + 0.5 * o[2]),
)


def tree(op, items):
    while len(items) > 1:
        items = [
            op(items[k], items[k + 1]) if k + 1 < len(items) else items[k]
            for k in range(0, len(items), 2)
        ]
    return items[0]


def stack_rows(pieces):
    return jnp.concatenate(pieces, axis=0)


def kernel(
    hidden_h, lengths_h, qkv_h, keys_h, values_h, outw_h, ids_h, comb_h, gate_h, down_h, rates_h,
    out_h,
    hidden_v, lengths_s, qkv_v, keys_v, values_v, ids_v, comb_v, gate_v, down_v, rates_v,
    qsend, qbuf, wbuf, asend, abuf, pick, rsend, rbuf, kept, hsend, hbuf,
    lsem, ssem, rsem,
):
    me = lax.axis_index("tp")
    x = lax.div(me, 8)
    z = lax.rem(lax.div(me, 2), 4)
    c = lax.rem(me, 2)

    def device(offset):
        dx, dz, dc = offset
        px = lax.rem(x + dx, 4) if dx else x
        pz = lax.rem(z + dz, 4) if dz else z
        pc = lax.rem(c + dc, 2) if dc else c
        return px, pz, pc

    def index(offset):
        px, pz, pc = device(offset)
        return px * 8 + pz * 2 + pc

    peers = [index(o) for o in PEERS]

    partner = me + 1 - 2 * c

    barrier = pltpu.get_barrier_semaphore()
    def greet(some):
        for p in some:
            pl.semaphore_signal(barrier, inc=1, device_id={"tp": p}, device_id_type=MESH)

    greet(peers[:10])

    def load(src, dst, i):
        copy = pltpu.make_async_copy(src, dst, lsem.at[i])
        copy.start()
        return copy

    c_hidden = load(hidden_h, hidden_v, 0)
    c_len = load(lengths_h, lengths_s, 1)
    c_qkv0 = load(qkv_h, qkv_v.at[pl.ds(0, 64)], 2)
    c_qkv1 = load(qkv_h, qkv_v.at[pl.ds(64, 64)], 3)
    c_rates = load(rates_h, rates_v, 4)
    greet(peers[10:])
    c_keys = load(keys_h, keys_v, 5)
    c_values = load(values_h, values_v, 6)
    c_ids = load(ids_h, ids_v, 7)
    c_comb = load(comb_h, comb_v, 8)
    c_gate = load(gate_h.at[0], gate_v.at[c], 9)
    own_half = pl.ds(pl.multiple_of(c * 512, 512), 512)
    other_half = pl.ds(pl.multiple_of(512 - c * 512, 512), 512)
    c_down = load(down_h.at[0, :, other_half], down_v.at[c], 10)

    def send(src, dst, phase, p):
        pltpu.make_async_remote_copy(
            src_ref=src, dst_ref=dst, send_sem=ssem.at[phase], recv_sem=rsem.at[phase],
            device_id={"tp": p}, device_id_type=MESH,
        ).start()

    def wait_bytes(ref, sem):
        pltpu.make_async_copy(ref, ref, sem).wait()

    sub = lax.broadcasted_iota(jnp.int32, (8, 128), 0)
    lane = lax.broadcasted_iota(jnp.int32, (8, 128), 1)
    low_half = lane < 64
    top_rows = sub < 4

    c_len.wait()
    lens = [lengths_s[r] for r in range(4)]
    c_rates.wait()
    front = jnp.where(top_rows, lens[0], lens[1])
    rear = jnp.where(top_rows, lens[2], lens[3])
    position = (jnp.where(low_half, front, rear) + jnp.bitwise_and(sub, 3)).astype(F32)
    angles = position * jnp.broadcast_to(rates_v[...], (8, 128))
    cosine = jnp.cos(angles)
    sine = jnp.sin(angles)
    c_hidden.wait()
    rows = stack_rows([hidden_v[r].astype(F32) for r in range(4)])
    normed = (
        rows * lax.rsqrt(jnp.mean(rows * rows, axis=-1, keepdims=True) + EPSILON)
    ).astype(BF16)
    c_qkv0.wait()
    c_qkv1.wait()
    head = lax.dot_general(
        normed, qkv_v[...], (((1,), (1,)), ((), ())), preferred_element_type=F32
    )
    head = head.astype(BF16).astype(F32)
    packed = jnp.where(low_half, head[0:8], head[8:16])
    ahead = pltpu.roll(packed, 96, 1)
    behind = pltpu.roll(packed, 32, 1)
    first = jnp.bitwise_and(lane, 63) < 32
    turned = packed * cosine + jnp.where(first, -ahead, behind) * sine
    turned = turned.astype(BF16).astype(F32)
    query = turned * 0.125
    place = jnp.broadcast_to(lax.rem(me, 4), (8, 128))
    query = jnp.where(place >= 2, pltpu.roll(query, 64, 1), query)
    query = jnp.where(jnp.bitwise_and(place, 1) == 1, pltpu.roll(query, 2, 0), query)
    query = jnp.where(place >= 2, pltpu.roll(query, 4, 0), query)
    whole_me = jnp.broadcast_to(me, (8, 128))
    qsend[...] = jnp.where(
        whole_me < 16, query, jnp.where(whole_me < 24, turned, packed)
    ).astype(BF16)
    for k in range(8):
        kept[k // 4, :, (k % 4) * 128 : (k % 4) * 128 + 128] = rows[:, k * 128 : k * 128 + 128]
    target = lax.broadcasted_iota(jnp.int32, (128, 512), 0)
    source = lax.broadcasted_iota(jnp.int32, (128, 512), 1)
    token = 2 * jnp.bitwise_and(lax.shift_right_logical(source, 4), 7) + jnp.bitwise_and(source, 1)
    column = jnp.bitwise_and(lax.shift_right_logical(source, 1), 7)
    pick[...] = jnp.where(target == column * 16 + token, 1.0, 0.0).astype(BF16)

    pl.semaphore_wait(barrier, 31)
    for p in peers:
        send(qsend, qbuf.at[me], 0, p)
    pltpu.make_async_copy(qsend, qbuf.at[me], rsem.at[0]).start()

    for dz in (2, 1, 3):
        send(outw_h, wbuf.at[2 * z + c], 1, x * 8 + lax.rem(z + dz, 4) * 2 + c)
    pltpu.make_async_copy(outw_h, wbuf.at[2 * z + c], rsem.at[1]).start()

    wait_bytes(qbuf, rsem.at[0])
    heads = [qbuf[h].astype(F32) for h in range(16)]
    pair = lax.shift_right_logical(sub, 1)
    mixed = []
    for q in range(4):
        row = []
        for n in range(4):
            tile = heads[4 * n + (3 - q) % 4]
            for p in range(3):
                tile = jnp.where(pair == p, heads[4 * n + (p - q) % 4], tile)
            row.append(tile)
        mixed.append(row)
    rear_head = [jnp.bitwise_and(pair - q, 3) >= 2 for q in range(4)]
    fits = [rear_head[q] != low_half for q in range(4)]
    c_keys.wait()
    c_values.wait()
    zero = jnp.zeros((8, 128), F32)
    all_scores = []
    for r in range(4):
        tiles = []
        for sp in range(2):
            q = 2 * (r % 2) + sp
            row = []
            for n in range(4):
                tile = mixed[q][n] if r < 2 else pltpu.roll(mixed[q][n], 64, 1)
                row.append(jnp.where(fits[q], tile, 0.0))
            tiles.append(row)
        columns = [
            jnp.concatenate(
                [tiles[sp][n] if n == k else zero for n in range(4) for sp in range(2)], axis=0
            )
            for k in range(4)
        ]
        queries = jnp.concatenate(columns, axis=1).astype(BF16)
        all_scores.append(
            lax.dot_general(
                queries, keys_v[r], (((1,), (1,)), ((), ())), preferred_element_type=F32
            )
        )
    cell = lax.broadcasted_iota(jnp.int32, (64, 128), 1) + me * 128
    live = [cell < lens[r] for r in range(4)]
    masked = [jnp.where(live[r], all_scores[r], NEGATIVE) for r in range(4)]
    peaks = [jnp.max(masked[r], axis=-1, keepdims=True) for r in range(4)]
    weights = [jnp.where(live[r], jnp.exp(masked[r] - peaks[r]), 0.0) for r in range(4)]
    sums = [
        jnp.dot(weights[r].astype(BF16), values_v[r], preferred_element_type=F32)
        for r in range(4)
    ]
    totals = [jnp.sum(weights[r], axis=-1, keepdims=True) for r in range(4)]
    for r in range(4):
        stats = jnp.where(
            lax.broadcasted_iota(jnp.int32, (64, 128), 1) < 96, peaks[r], totals[r]
        )
        for n in range(4):
            for sp in range(2):
                b = 8 * (2 * n + sp)
                o = sums[r][b : b + 8, n * 128 : n * 128 + 128]
                o = jnp.where(rear_head[2 * (r % 2) + sp], pltpu.roll(o, 64, 1), o)
                asend[n * 8 + r * 2 + sp] = jnp.where(low_half, o, stats[b : b + 8])

    for p in peers:
        send(asend.at[p], abuf.at[me], 2, p)
    pltpu.make_async_copy(asend.at[me], abuf.at[me], rsem.at[2]).start()

    wait_bytes(wbuf.at[pl.ds(0, 4)], rsem.at[1])
    for k in range(4):
        send(wbuf.at[2 * k + c], wbuf.at[2 * k + c], 3, partner)

    send(gate_h.at[0], gate_v.at[c], 5, partner)
    send(down_h.at[0, :, own_half], down_v.at[c], 8, partner)

    late = jnp.broadcast_to(lax.rem(z, 2), (8, 128)) == 1
    rear_half = jnp.broadcast_to(lax.div(z, 2), (8, 128)) == 1
    q_own = 2 * lax.rem(z, 2) + c
    tile = qbuf[4 * x + lax.rem(7 - q_own, 4)].astype(F32)
    for p in range(3):
        tile = jnp.where(pair == p, qbuf[4 * x + lax.rem(p + 4 - q_own, 4)].astype(F32), tile)
    head_place = jnp.bitwise_and(pair - jnp.broadcast_to(q_own, (8, 128)), 3)
    own_rear = head_place >= 2
    own_queries = jnp.where(
        low_half, jnp.where(own_rear != rear_half, pltpu.roll(tile, 64, 1), tile), 0.0
    )

    def own_rows(i):
        v = qbuf[i].astype(F32)
        v = jnp.where(rear_half, pltpu.roll(v, 64, 1), v)
        return jnp.where(late, pltpu.roll(v, 4, 0), v)

    def per_head(front, rear):
        return [
            jnp.where(
                own_rear,
                jnp.broadcast_to(rear[s : s + 1], (8, 128)),
                jnp.broadcast_to(front[s : s + 1], (8, 128)),
            )
            for s in range(4)
        ]

    new_keys = per_head(own_rows(16 + 2 * x), own_rows(17 + 2 * x))
    new_values = per_head(own_rows(24 + 2 * x), own_rows(25 + 2 * x))
    step = 2 * jnp.broadcast_to(c, (8, 128)) + jnp.bitwise_and(sub, 1)
    new_scores = []
    for s in range(4):
        score = jnp.sum(
            own_queries * new_keys[s], axis=-1, keepdims=True
        )
        new_scores.append(
            jnp.where(step >= s, jnp.broadcast_to(score, (8, 128)), NEGATIVE)
        )
    new_peak = functools.reduce(jnp.maximum, new_scores)
    new_weights = [jnp.exp(v - new_peak) for v in new_scores]
    new_total = functools.reduce(jnp.add, new_weights)
    new_sum = functools.reduce(
        jnp.add,
        [
            new_weights[s].astype(BF16).astype(F32) * new_values[s]
            for s in range(4)
        ],
    )
    c_ids.wait()
    c_comb.wait()
    factors = [
        stack_rows(
            [
                jnp.sum(
                    jnp.where(ids_v[r] == me - c + e, comb_v[r], 0).astype(F32),
                    axis=-1,
                    keepdims=True,
                )
                for r in range(4)
            ]
        )
        * (1.0 / 65536.0)
        for e in range(2)
    ]
    wait_bytes(wbuf.at[pl.ds(0, 4)], rsem.at[3])

    wait_bytes(abuf, rsem.at[2])
    peaks = [jnp.broadcast_to(abuf[b][:, 64:65], (8, 128)) for b in range(32)]
    top = tree(jnp.maximum, peaks + [new_peak])
    total_all = tree(jnp.add, [jnp.exp(peaks[b] - top) * abuf[b] for b in range(32)])
    carried = jnp.exp(new_peak - top)
    denominator = jnp.broadcast_to(total_all[:, 96:97], (8, 128)) + carried * new_total
    attended = jnp.where(low_half, (total_all + carried * new_sum) / denominator, 0.0)
    attended = attended + pltpu.roll(attended, 64, 1)
    half = lax.shift_right_logical(lane, 6)
    attended = jnp.concatenate(
        [
            jnp.where(half == head_place, attended, 0.0),
            jnp.where(half + 2 == head_place, attended, 0.0),
        ],
        axis=1,
    ).astype(BF16)
    product = jnp.dot(
        attended, wbuf[...].reshape(256, 1024), preferred_element_type=F32
    )
    product = product + pltpu.roll(product, 4, 0)
    product = product + pltpu.roll(product, 2, 0)
    parts = []
    for m in range(2):
        part = product[:, m * 512 + 384 : m * 512 + 512]
        for k in range(3):
            at = m * 512 + k * 128
            part = jnp.where(pair == k, product[:, at : at + 128], part)
        parts.append(part)
    rsend[...] = jnp.concatenate(parts, axis=0).astype(BF16)
    for p in peers:
        send(rsend, rbuf.at[me], 4, p)
    pltpu.make_async_copy(rsend, rbuf.at[me], rsem.at[4]).start()
    c_gate.wait()
    c_down.wait()
    wait_bytes(rbuf, rsem.at[4])
    projected = jnp.dot(
        pick[...], rbuf[...].reshape(512, 128), preferred_element_type=F32
    )
    rows = []
    for k in range(8):
        at = pl.ds((k % 4) * 128, 128)
        row = kept[k // 4, :, at] + projected[16 * k : 16 * k + 16]
        kept[k // 4, :, at] = row
        rows.append(row)
    rows = jnp.concatenate(rows, axis=1)
    normed = (
        rows * lax.rsqrt(jnp.mean(rows * rows, axis=-1, keepdims=True) + EPSILON)
    ).astype(BF16)
    wait_bytes(gate_v.at[0], rsem.at[5])
    wait_bytes(down_v.at[0], rsem.at[8])
    activations = []
    for e in range(2):
        united = jnp.dot(normed, gate_v[e], preferred_element_type=F32)
        gate = united[:, :512]
        activations.append(
            (gate / (1.0 + jnp.exp(-gate)) * united[:, 512:] * factors[e]).astype(BF16)
        )
    hsend[...] = jnp.dot(
        jnp.concatenate(activations, axis=1),
        down_v[...].reshape(1024, 512),
        preferred_element_type=F32,
    ).astype(BF16)
    chip = 4 * x + z
    for o in PEERS:
        if o[2] == 1:
            send(hsend, hbuf.at[chip], 6, index(o))
    wait_bytes(hbuf, rsem.at[6])
    final = kept[c] + tree(jnp.add, [hbuf[k].astype(F32) for k in range(16)])
    for r in range(4):
        out_h[r, :, own_half] = final[4 * r : 4 * r + 4].astype(BF16)
    send(out_h.at[:, :, own_half], out_h.at[:, :, own_half], 7, partner)
    wait_bytes(out_h.at[:, :, other_half], rsem.at[7])

    wait_bytes(qbuf.at[pl.ds(0, 31)], ssem.at[0])
    wait_bytes(wbuf.at[pl.ds(0, 3)], ssem.at[1])
    wait_bytes(abuf.at[pl.ds(0, 31)], ssem.at[2])
    wait_bytes(wbuf.at[pl.ds(0, 4)], ssem.at[3])
    wait_bytes(rbuf.at[pl.ds(0, 31)], ssem.at[4])
    wait_bytes(gate_v.at[0], ssem.at[5])
    wait_bytes(down_v.at[0], ssem.at[8])
    wait_bytes(hbuf, ssem.at[6])
    wait_bytes(out_h.at[:, :, own_half], ssem.at[7])


def per_device(*args):
    half = np.arange(128) % 32
    rates = (ROPE_BASE ** (-2.0 * half / 64.0)).astype(np.float32)
    anywhere = pl.BlockSpec(memory_space=pl.ANY)
    return pl.pallas_call(
        kernel,
        out_shape=pltpu.VMEM((4, 4, 1024), BF16),
        in_specs=[anywhere] * 11,
        out_specs=pl.BlockSpec(memory_space=pltpu.VMEM),
        scratch_shapes=[
            pltpu.VMEM((4, 4, 1024), BF16),
            pltpu.SMEM((4,), jnp.int32),
            pltpu.VMEM((128, 1024), BF16),
            pltpu.VMEM((4, 128, 512), BF16),
            pltpu.VMEM((4, 128, 512), BF16),
            pltpu.VMEM((4, 4, 8), jnp.int32),
            pltpu.VMEM((4, 4, 8), jnp.int32),
            pltpu.VMEM((2, 1024, 1024), BF16),
            pltpu.VMEM((2, 512, 512), BF16),
            pltpu.VMEM((1, 128), F32),
            pltpu.VMEM((8, 128), BF16),
            pltpu.VMEM((32, 8, 128), BF16),
            pltpu.VMEM((8, 32, 1024), BF16),
            pltpu.VMEM((32, 8, 128), F32),
            pltpu.VMEM((32, 8, 128), F32),
            pltpu.VMEM((128, 512), BF16),
            pltpu.VMEM((16, 128), BF16),
            pltpu.VMEM((32, 16, 128), BF16),
            pltpu.VMEM((2, 16, 512), F32),
            pltpu.VMEM((16, 512), BF16),
            pltpu.VMEM((16, 16, 512), BF16),
            pltpu.SemaphoreType.DMA((11,)),
            pltpu.SemaphoreType.DMA((9,)),
            pltpu.SemaphoreType.DMA((9,)),
        ],
        compiler_params=pltpu.CompilerParams(collective_id=0, has_side_effects=True),
        name="decoder_layer",
    )(*args, jnp.asarray(rates).reshape(1, 128))


def solution(mesh):
    in_specs = (
        P("req", None, None),
        P("req"),
        P("tp", None),
        P("req", "tp", None),
        P("req", "tp", None),
        P("tp", None),
        P("req", None, None),
        P("req", None, None),
        P("tp", None, None),
        P("tp", None, None),
    )
    out_specs = P("req", None, None)
    return jax.shard_map(
        per_device, mesh=mesh, in_specs=in_specs, out_specs=out_specs, check_vma=False
    )
```
